32 devices in a mesh: grid: 4 (over z), basis: 8 (over y, x, core).
Axes of the slice: x: 2, y: 2, z: 4, core: 2. Of those that a mesh axis runs over, the one named last changes fastest.
Arguments:
- basis_values: bfloat16 [512, 256, 512], P(('grid', 'basis')), may hold values from -6 to 6
- weights: float32 [512, 256], P(('grid', 'basis')), may hold values from 0.1 to 1
- points: bfloat16 [512, 3, 256], P(('grid', 'basis')), may hold values from 0 to 1
- block_lists: int32 [512, 4], P(('grid', 'basis')), may hold values from 0 to 31, as said below
- counts: int32 [8, 4], P('basis', 'grid'), may hold values from 1 to 16, 32 in all within a row
- density: bfloat16 [4096, 4096], P('basis'), may hold values from -0.25 to 0.25
- centers: float32 [3, 4096], replicated, may hold values from 0 to 1
- block_centers: float32 [3, 32], replicated, may hold values from 0 to 1
- block_exponents: float32 [32], replicated, may hold values from 2 to 20
Outputs:
- exchange_matrix: float32 [4096, 4096], P('basis', 'grid')
The draws below stay inside these ranges and needn't reach their ends.
Inputs may be any that keep to these rules, and one draw needn't show every extreme that they name: `block_lists`: each row names 4 different blocks. The rows of all devices with the same basis index name together exactly 8 different blocks, consecutive ones counted on from 31 to 0, and the rows of each such device name all 8 of them; one of them is named by every row of those devices. The blocks of basis index 0 begin at block 31. Entry [b, g] counts the live batches of the device at grid index g and basis index b, which are its first ones. Each row sums to 32 and its largest entry is 16.
All inputs are finite; a program needn't handle non-finite values.
Results may differ from the reference program's by a relative error of at most 0.0018.
Values may be sent and summed in bfloat16 or wider, within the bound.
A program may use at most 128 MiB of HBM per device.

```python
import math
import jax
import jax.numpy as jnp
import numpy as np
from jax import lax

TB = 128
LB = 4
CL = 8
P_SIZE = 256
BAT_DEV = 16
L = 512
NBLK = 32
NB = 4096
NBAT = 512
N_GRID = 4
N_BASIS = 8


def draw_block_lists(key, part):
    device_total = N_GRID * N_BASIS
    row_total = BAT_DEV * device_total
    others = CL - 1
    picked_count = LB - 1
    cover_rows = (others + picked_count - 1) // picked_count
    start_keys = jax.random.split(jax.random.fold_in(key, 11), 6)
    first_block = jax.random.randint(start_keys[0], (N_BASIS,), 0, NBLK)
    first_block = first_block.at[0].set(NBLK - 1)
    core_place = jax.random.randint(start_keys[1], (N_BASIS,), 0, CL)
    shuffle_others = jax.vmap(lambda chosen: jax.random.permutation(chosen, others))(jax.random.split(start_keys[2], N_BASIS))
    row_orders = jax.vmap(lambda chosen: jax.random.permutation(chosen, BAT_DEV))(jax.random.split(start_keys[3], device_total))
    free_offset = jax.random.randint(start_keys[4], (row_total,), 0, others)
    rotation = jax.random.randint(start_keys[5], (row_total,), 0, LB)
    row_index = jnp.arange(row_total, dtype=jnp.int32)
    device_at = row_index // BAT_DEV
    basis_at = device_at % N_BASIS
    ranked = row_orders[device_at, row_index % BAT_DEV]
    offset_at = jnp.where(ranked < cover_rows, ranked * picked_count, free_offset)
    steps_along = jnp.arange(picked_count, dtype=jnp.int32)
    other_slot = shuffle_others[basis_at[:, None], (offset_at[:, None] + steps_along[None, :]) % others]
    core_here = core_place[basis_at][:, None]
    cluster_slot = other_slot + (other_slot >= core_here).astype(jnp.int32)
    listed_slot = jnp.concatenate([core_here, cluster_slot], axis=1)
    turned = (jnp.arange(LB, dtype=jnp.int32)[None, :] + rotation[:, None]) % LB
    listed_slot = jnp.take_along_axis(listed_slot, turned, axis=1)
    return ((first_block[basis_at][:, None] + listed_slot) % NBLK).astype(jnp.int32)


def levels(stream_key, extent, cuts, least, high):
    gain, own = 1.0, jax.random.fold_in(stream_key, 6)
    for dim, blocks in cuts:
        heights = jnp.exp(jax.random.uniform(jax.random.fold_in(own, dim), (blocks,), jnp.float32, least / len(cuts), high / len(cuts)))
        gain = gain * jnp.repeat(heights, extent[dim] // blocks).reshape([-1 if axis == dim else 1 for axis in range(len(extent))])
    return gain


def split_up(count, total, limit, slope):
    weights = [(1 << 20) // math.isqrt(rank ** slope) + 1 for rank in range(2, count + 1)]
    rest, holding = total - limit - (count - 1), [1] * (count - 1)
    while rest > 0:
        candidates = [i for i in range(count - 1) if holding[i] < limit]
        whole, left = sum([weights[i] for i in candidates]), rest
        for i in candidates:
            extra = min(limit - holding[i], max(1, left * weights[i] // whole), rest)
            holding[i] = holding[i] + extra
            rest = rest - extra
    return np.array([limit] + holding)


def uneven(key, amount, total, most, skew):
    if amount == 2:
        one = jax.random.randint(key, (), max(1, total - most), min(most, total - 1) + 1)
        return jnp.stack([one, total - one])
    tallies = jnp.asarray(split_up(amount, total, most, skew), jnp.int32)
    couples = (amount - 1) // 2
    source_of, receiver = tallies[1:1 + 2 * couples:2], tallies[2:2 + 2 * couples:2]
    slack = jnp.minimum(source_of - 1, most - receiver)
    moved = jax.random.randint(jax.random.fold_in(key, 1), (couples,), 0, 1 << 20) % (slack + 1)
    tallies = tallies.at[1:1 + 2 * couples:2].set(source_of - moved).at[2:2 + 2 * couples:2].set(receiver + moved)
    return tallies[jax.random.permutation(jax.random.fold_in(key, 2), amount)]


def normal_values(key, dims, width, limit, cuts=(), kind=jnp.bfloat16):
    result = jax.random.normal(key, dims, jnp.float32) * width
    if len(cuts) > 0:
        result = levels(key, dims, cuts, -0.22, 0.18) * result
    return jnp.clip(result, min=-limit, max=limit).astype(kind)


def setup_inputs(seed: int = 0) -> dict:
    seeds = jax.random.split(jax.random.key(seed), 10)
    return {
        "basis_values": normal_values(seeds[0], (NBAT, P_SIZE, L), 1.0, 6.0, ((0, 32),)),
        "weights": jnp.clip(jnp.exp(math.log(1.0) - 2.3025851 * jax.random.uniform(seeds[1], (NBAT, P_SIZE), jnp.float32) ** levels(seeds[1], (NBAT, P_SIZE), ((0, 32),), -0.2, 0.2)), 0.1, 1.0),
        "points": jnp.clip(1.0 * jax.random.uniform(seeds[2], (NBAT, 3, P_SIZE), jnp.float32) ** levels(seeds[2], (NBAT, 3, P_SIZE), ((0, 32),), -0.2, 0.2), 0.0, 1.0).astype(jnp.bfloat16),
        "block_lists": draw_block_lists(jax.random.fold_in(seeds[9], 71), 0),
        "counts": jax.vmap(lambda own: uneven(own, N_GRID, N_GRID * BAT_DEV // 2, BAT_DEV, 2))(jax.random.split(seeds[4], N_BASIS)).reshape((N_BASIS, N_GRID)).astype(jnp.int32),
        "density": normal_values(seeds[5], (NB, NB), L ** -0.5, 0.25, ((0, 8),)),
        "centers": jnp.clip(jax.random.uniform(seeds[6], (3, NB), jnp.float32, 0.0, 1.0), 0.0, 1.0),
        "block_centers": jnp.clip(jax.random.uniform(seeds[7], (3, NBLK), jnp.float32, 0.0, 1.0), 0.0, 1.0),
        "block_exponents": jnp.clip(jnp.exp(jax.random.uniform(seeds[8], (NBLK,), jnp.float32, math.log(2.0), math.log(20.0))), 2.0, 20.0),
    }


def boys_single(points_f, blocks, block_centers, block_exponents):
    centre = block_centers[:, blocks]
    middle = 0.5 * (centre[:, :, None] + centre[:, None, :])
    exponents = block_exponents[blocks]
    rate_pair = 0.5 * (exponents[:, None] + exponents[None, :])
    offset = points_f[:, None, None, :] - middle[:, :, :, None]
    distance = lax.optimization_barrier(jnp.sum(offset * offset, axis=0))
    tau_value = rate_pair[:, :, None] * distance + 0.05
    root_value = jnp.sqrt(tau_value)
    return 0.5 * math.sqrt(math.pi) * lax.erf(root_value) / root_value

def coupling_single(blocks, centers):
    functions = (blocks[:, None] * TB + jnp.arange(TB, dtype=jnp.int32)[None, :]).reshape(L)
    where_at = centers[:, functions]
    spread = where_at[:, :, None] - where_at[:, None, :]
    distance = lax.optimization_barrier(jnp.sum(spread * spread, axis=0))
    sharpness = float(NB) ** (2.0 / 3.0)
    return jnp.exp(-sharpness * distance).astype(jnp.bfloat16)

def reference(basis_values, weights, points, block_lists, counts, density, centers, block_centers, block_exponents):
    density_tiles = density.reshape(NBLK, TB, NBLK, TB)

    def one_batch(accumulated, index):
        blocks = block_lists[index]
        grid_at = index // (N_BASIS * BAT_DEV)
        basis_at = index // BAT_DEV % N_BASIS
        within = index % BAT_DEV
        is_live = within < counts[basis_at, grid_at]
        dens_list = density_tiles[blocks[:, None], :, blocks[None, :], :]
        dens_list = dens_list.transpose(0, 2, 1, 3).reshape(L, L)
        values = basis_values[index]
        mapped = jnp.dot(values, dens_list.T, preferred_element_type=jnp.float32).astype(jnp.bfloat16)
        coupled = coupling_single(blocks, centers).reshape(LB, TB, LB, TB)
        partial_rows = jnp.einsum('puj,tiuj->ptui', mapped.reshape(P_SIZE, LB, TB).astype(jnp.float32), coupled.astype(jnp.float32), precision=lax.Precision.HIGHEST)
        factor = boys_single(points[index].astype(jnp.float32), blocks, block_centers, block_exponents)
        boys_weight = factor.transpose(2, 0, 1)[:, :, :, None]
        potential = lax.optimization_barrier(jnp.sum(partial_rows * boys_weight, axis=2)).astype(jnp.bfloat16).reshape(P_SIZE, L)
        scaled = jnp.where(is_live, weights[index], 0.0) / P_SIZE
        weighted = (values * scaled[:, None]).astype(jnp.bfloat16)
        batch_tile = jnp.dot(weighted.T, potential, preferred_element_type=jnp.float32)
        update = batch_tile.reshape(LB, TB, LB, TB).transpose(0, 2, 1, 3)
        accumulated = accumulated.at[blocks[:, None], :, blocks[None, :], :].add(update)
        return (accumulated, None)
    start_value = jnp.zeros((NBLK, TB, NBLK, TB), jnp.float32)
    accumulated, unused = lax.scan(one_batch, start_value, jnp.arange(NBAT, dtype=jnp.int32))
    return accumulated.reshape(NB, NB)
```

```python
import functools
import math

import jax
import jax.numpy as jnp
from jax import lax
from jax.experimental import pallas as pl
from jax.experimental.pallas import tpu as pltpu
from jax.sharding import PartitionSpec as P

TB = 128
CL = 8
MESH = pl.DeviceIdType.MESH


def greet(me_grid, me_basis, grid_size, basis_size):
    barrier = pltpu.get_barrier_semaphore()
    for d in range(1, grid_size):
        pl.semaphore_signal(
            barrier,
            inc=1,
            device_id=(lax.rem(me_grid + d, grid_size), me_basis),
            device_id_type=MESH,
        )
    for d in range(1, basis_size):
        pl.semaphore_signal(
            barrier,
            inc=1,
            device_id=(me_grid, lax.rem(me_basis + d, basis_size)),
            device_id_type=MESH,
        )


def greeted(grid_size, basis_size):
    pl.semaphore_wait(pltpu.get_barrier_semaphore(), grid_size + basis_size - 2)


def prepare_kernel(
    grid_size,
    basis_size,
    owned,
    parts,
    lists_ref,
    count_ref,
    bc_ref,
    be_ref,
    weights_ref,
    points_ref,
    centers_ref,
    values_hbm,
    density_hbm,
    dens_out,
    coup_out,
    boys_out,
    weighted_out,
    firsts_out,
    values_v,
    density_v,
    packed,
    *scratch,
):
    per = CL // grid_size
    rows = TB // parts
    chunks = per * parts
    landed = scratch[:chunks]
    first_v, firsts_s, wcol, cols, places, local_sems, d_sems = scratch[chunks : chunks + 7]
    f_send, f_recv, x_send, x_recv, z_send, z_recv = scratch[chunks + 7 :]
    batches, lists = lists_ref.shape
    block_count = be_ref.shape[0]
    point_total = weights_ref.shape[1]
    me_grid = lax.axis_index("grid")
    me_basis = lax.axis_index("basis")

    greet(me_grid, me_basis, grid_size, basis_size)
    def density_in(c):
        return pltpu.make_async_copy(
            density_hbm.at[:, c * TB : (c + 1) * TB], density_v.at[c], d_sems.at[c]
        )

    for c in range(block_count):
        density_in(c).start()
    values_in = pltpu.make_async_copy(values_hbm, values_v, local_sems.at[1])
    values_in.start()
    for c in range(block_count):
        places[c] = centers_ref[:, c * TB : (c + 1) * TB]

    half = block_count // 2
    origin = lists_ref[0, 0]
    low = jnp.int32(0)
    for b in range(batches):
        for t in range(lists):
            shift = lax.rem(lists_ref[b, t] - origin + block_count + half, block_count) - half
            low = jnp.minimum(low, shift)
    first = lax.rem(origin + low + block_count, block_count)
    first_v[...] = jnp.full(first_v.shape, first, jnp.int32)
    firsts_out[0] = jnp.full(firsts_out.shape[1:], first, jnp.int32)

    def member(begin, residue):
        return lax.rem(begin + ((residue - begin) & (CL - 1)), block_count)

    greeted(grid_size, basis_size)

    def f_copy(d):
        return pltpu.make_async_remote_copy(
            src_ref=first_v,
            dst_ref=firsts_out.at[d],
            send_sem=f_send.at[d - 1],
            recv_sem=f_recv.at[d - 1],
            device_id=(me_grid, lax.rem(me_basis + d, basis_size)),
            device_id_type=MESH,
        )

    for d in range(1, basis_size):
        f_copy(d).start()

    members = [member(first, r) for r in range(CL)]
    stacked = jnp.concatenate(
        [places[m] for m in members] + [jnp.zeros((TB - 3 * CL, TB), jnp.float32)], axis=0
    )
    cols[...] = stacked.T
    live = lax.broadcasted_iota(jnp.int32, weights_ref.shape, 0) < count_ref[0, 0]
    scaled = jnp.where(live, weights_ref[...], 0.0) / point_total
    scaled = jnp.concatenate(
        [scaled, jnp.zeros((TB - batches, point_total), jnp.float32)], axis=0
    )
    wcol[...] = scaled.T

    for d in range(1, basis_size):
        f_copy(d).wait_recv()
    firsts_in = pltpu.make_async_copy(firsts_out, firsts_s, local_sems.at[2])
    firsts_in.start()
    for c in range(block_count):
        density_in(c).wait()
    firsts_in.wait()

    def x_copy(k, d):
        return pltpu.make_async_remote_copy(
            src_ref=packed.at[d, k],
            dst_ref=landed[k].at[d],
            send_sem=x_send.at[d - 1, k],
            recv_sem=x_recv.at[d - 1, k],
            device_id=(me_grid, lax.rem(me_basis + d, basis_size)),
            device_id_type=MESH,
        )

    def z_copy(k, j, side):
        cc, part = k // parts, k % parts
        at = (j, cc, slice(None), pl.ds(part * rows, rows))
        return pltpu.make_async_remote_copy(
            src_ref=dens_out.at[at],
            dst_ref=dens_out.at[at],
            send_sem=z_send.at[j, k, side],
            recv_sem=z_recv.at[j, k],
            device_id=(me_grid + 1 if side == 0 else me_grid - 1, me_basis),
            device_id_type=MESH,
        )

    def pack(k, d):
        cc, part = k // parts, k % parts
        begin = firsts_s[lax.rem(basis_size - d, basis_size), 0, 0]
        if d == 0:
            column = member(first, me_grid * per + cc)
        else:
            column = member(begin, me_grid * per + cc)
        for i in range(owned):
            block = density_v[column, i * TB + part * rows : i * TB + (part + 1) * rows, :]
            if d == 0:
                landed[k][0, i] = block
            else:
                packed[d, k, i] = block

    slots = [lax.rem(me_basis - m // owned + basis_size, basis_size) for m in members]

    def own(k):
        cc, part = k // parts, k % parts
        for d in range(1, basis_size):
            x_copy(k, d).wait_recv()
        for r in range(CL):
            dens_out[me_grid, cc, r, part * rows : (part + 1) * rows, :] = landed[k][
                slots[r], r % owned
            ]

        @pl.when(me_grid < grid_size - 1)
        def _():
            z_copy(k, me_grid, 0).start()

        @pl.when(me_grid > 0)
        def _():
            z_copy(k, me_grid, 1).start()

    def relay(k, h):
        @pl.when(me_grid >= h)
        def _():
            z_copy(k, me_grid - h, 0).wait_recv()

            @pl.when(me_grid < grid_size - 1)
            def _():
                z_copy(k, me_grid - h, 0).start()

        @pl.when(me_grid + h < grid_size)
        def _():
            z_copy(k, me_grid + h, 1).wait_recv()

            @pl.when(me_grid > 0)
            def _():
                z_copy(k, me_grid + h, 1).start()

    sharpness = float(centers_ref.shape[1]) ** (2.0 / 3.0)

    def couple(r):
        mine = [cols[:, 3 * r + d : 3 * r + d + 1] for d in range(3)]
        for u in range(CL):
            other = places[members[u]]
            spread = [mine[d] - other[d : d + 1] for d in range(3)]
            distance = spread[0] * spread[0] + spread[1] * spread[1] + spread[2] * spread[2]
            coup_out[r, u] = jnp.exp(-sharpness * distance).astype(jnp.bfloat16)

    pair_shape = (lists * lists, point_total)
    t_at = lax.broadcasted_iota(jnp.int32, pair_shape, 0) // lists
    u_at = lax.broadcasted_iota(jnp.int32, pair_shape, 0) % lists

    def weigh(b):
        weighted_out[b] = (values_v[b].astype(jnp.float32) * wcol[:, b : b + 1]).astype(
            jnp.bfloat16
        )
        blocks = [lists_ref[b, t] for t in range(lists)]

        def spread_out(numbers, at):
            result = jnp.full(pair_shape, numbers[0], jnp.float32)
            for t in range(1, lists):
                result = jnp.where(at == t, numbers[t], result)
            return result

        distance = None
        for d in range(3):
            numbers = [bc_ref[d, block] for block in blocks]
            middle = 0.5 * (spread_out(numbers, t_at) + spread_out(numbers, u_at))
            offset = points_ref[b, d : d + 1, :].astype(jnp.float32) - middle
            square = offset * offset
            distance = square if distance is None else distance + square
        numbers = [be_ref[block] for block in blocks]
        rate = 0.5 * (spread_out(numbers, t_at) + spread_out(numbers, u_at))
        tau = rate * distance + 0.05
        root = jnp.sqrt(tau)
        boys_out[b] = 0.5 * math.sqrt(math.pi) * lax.erf(root) / root

    work = [functools.partial(couple, r) for r in range(CL)]
    work += [functools.partial(weigh, b) for b in range(batches)]
    share = -(-len(work) // chunks)

    for k in range(chunks):
        for d in range(1, basis_size):
            pack(k, d)
            x_copy(k, d).start()
    for k in range(chunks):
        pack(k, 0)
    values_in.wait()
    for k in range(chunks + grid_size):
        for piece in work[k * share : (k + 1) * share]:
            piece()
        if k < chunks:
            own(k)
        for h in range(1, grid_size):
            if 0 <= k - h < chunks:
                relay(k - h, h)

    for d in range(1, basis_size):
        f_copy(d).wait_send()
    for k in range(chunks):
        for d in range(1, basis_size):
            x_copy(k, d).wait_send()
        for h in range(grid_size):

            @pl.when((me_grid >= h) & (me_grid < grid_size - 1))
            def _():
                z_copy(k, me_grid - h, 0).wait_send()

            @pl.when((me_grid + h < grid_size) & (me_grid > 0))
            def _():
                z_copy(k, me_grid + h, 1).wait_send()


def prepare(
    values, weights, points, block_lists, counts, density, centers, block_centers, block_exponents,
    grid_size, basis_size, owned,
):
    per = CL // grid_size
    parts = 4 // per
    chunks = per * parts
    batches, point_total, listed = values.shape
    lists = block_lists.shape[1]
    block_count = block_exponents.shape[0]
    vmem = pl.BlockSpec(memory_space=pltpu.VMEM)
    smem = pl.BlockSpec(memory_space=pltpu.SMEM)
    anywhere = pl.BlockSpec(memory_space=pl.ANY)
    message = (owned, TB // parts, TB)
    dma = pltpu.SemaphoreType.DMA
    return pl.pallas_call(
        functools.partial(prepare_kernel, grid_size, basis_size, owned, parts),
        out_shape=[
            jax.ShapeDtypeStruct((grid_size, per, CL, TB, TB), jnp.bfloat16),
            jax.ShapeDtypeStruct((CL, CL, TB, TB), jnp.bfloat16),
            jax.ShapeDtypeStruct((batches, lists * lists, point_total), jnp.float32),
            jax.ShapeDtypeStruct(values.shape, jnp.bfloat16),
            jax.ShapeDtypeStruct((basis_size, 1, TB), jnp.int32),
        ],
        in_specs=[smem] * 4 + [vmem] * 3 + [anywhere] * 2,
        out_specs=[vmem] * 5,
        scratch_shapes=[
            pltpu.VMEM(values.shape, jnp.bfloat16),
            pltpu.VMEM((block_count, density.shape[0], TB), jnp.bfloat16),
            pltpu.VMEM((basis_size, chunks) + message, jnp.bfloat16),
            *[pltpu.VMEM((basis_size,) + message, jnp.bfloat16) for k in range(chunks)],
            pltpu.VMEM((1, TB), jnp.int32),
            pltpu.SMEM((basis_size, 1, TB), jnp.int32),
            pltpu.VMEM((point_total, TB), jnp.float32),
            pltpu.VMEM((TB, TB), jnp.float32),
            pltpu.VMEM((block_count, 3, TB), jnp.float32),
            dma((3,)),
            dma((block_count,)),
            dma((basis_size - 1,)),
            dma((basis_size - 1,)),
            dma((basis_size - 1, chunks)),
            dma((basis_size - 1, chunks)),
            dma((grid_size, chunks, 2)),
            dma((grid_size, chunks)),
        ],
        compiler_params=pltpu.CompilerParams(
            collective_id=1, has_side_effects=True, vmem_limit_bytes=32 * 1024 * 1024
        ),
        name="prepare",
    )(
        block_lists, counts, block_centers, block_exponents, weights, points, centers, values,
        density,
    )


def region_kernel(
    per, group, lists_ref, count_ref, values_ref, weighted_ref, boys_ref, dens_ref, coup_ref, acc
):
    lists = lists_ref.shape[1]
    acc[...] = jnp.zeros_like(acc)

    def one(b):
        at = [lists_ref[b, t] & (CL - 1) for t in range(lists)]
        dens = jnp.concatenate(
            [
                jnp.concatenate([dens_ref[c // per, c % per, r] for c in at], axis=1)
                for r in at
            ],
            axis=0,
        )
        mapped = lax.dot_general(
            dens, values_ref[b], (((1,), (1,)), ((), ())), preferred_element_type=jnp.float32
        ).astype(jnp.bfloat16)
        total = None
        for u in range(lists):
            coup = jnp.concatenate([coup_ref[r, at[u]] for r in at], axis=0)
            part = jnp.dot(
                coup, mapped[u * TB : (u + 1) * TB], preferred_element_type=jnp.float32
            )
            part = jnp.concatenate(
                [
                    part[t * TB : (t + 1) * TB]
                    * boys_ref[b, pl.ds(t * lists + u, 1), :]
                    for t in range(lists)
                ],
                axis=0,
            )
            total = part if total is None else total + part
        tile = jnp.dot(
            total.astype(jnp.bfloat16), weighted_ref[b], preferred_element_type=jnp.float32
        )
        return at, tile

    def step(n, carry):
        for at, tile in [one(n * group + b) for b in range(group)]:
            for c in range(lists):
                for r in range(lists):
                    acc[at[c], at[r]] += tile[c * TB : (c + 1) * TB, r * TB : (r + 1) * TB]
        return carry

    lax.fori_loop(0, (count_ref[0, 0] + group - 1) // group, step, 0)


def region_exchange(block_lists, counts, values, weighted, boys, dens, coup, grid_size):
    group = math.gcd(values.shape[0], 2)
    vmem = pl.BlockSpec(memory_space=pltpu.VMEM)
    smem = pl.BlockSpec(memory_space=pltpu.SMEM)
    return pl.pallas_call(
        functools.partial(region_kernel, CL // grid_size, group),
        in_specs=[smem] * 2 + [vmem] * 5,
        out_specs=vmem,
        out_shape=jax.ShapeDtypeStruct((CL, CL, TB, TB), jnp.float32),
        compiler_params=pltpu.CompilerParams(vmem_limit_bytes=32 * 1024 * 1024),
        name="region_exchange",
    )(block_lists, counts, values, weighted, boys, dens, coup)


def encode(tile):
    top = jnp.maximum(jnp.max(jnp.abs(tile), axis=0, keepdims=True), 1e-30)
    steps = jnp.round(tile * (32767.0 / top))
    return steps.astype(jnp.int32).astype(jnp.int16), top * (1.0 / 32767.0)


def decode(coded, scale):
    return coded.astype(jnp.int32).astype(jnp.float32) * scale


def collect_kernel(
    grid_size,
    basis_size,
    owned,
    turns,
    halves,
    acc,
    firsts,
    out,
    kq,
    ks,
    lq,
    ls,
    rq,
    rs,
    sq,
    ss,
    xq,
    xs,
    hq,
    hs,
    wq,
    ws,
    r_send,
    l_recv,
    r_recv,
    x_send,
    x_recv,
    w_send,
    w_recv,
):
    per = CL // grid_size
    members = CL // owned
    per_owner = turns * per
    width = owned // halves
    units = per * halves
    tiles = members * width
    block_count = turns * CL
    me_grid = lax.axis_index("grid")
    me_basis = lax.axis_index("basis")
    mine = lax.rem(me_basis, members)

    greet(me_grid, me_basis, grid_size, basis_size)
    greeted(grid_size, basis_size)

    def pair(sources, targets, sends, recvs, device):
        return [
            pltpu.make_async_remote_copy(
                src_ref=sources[which],
                dst_ref=targets[which],
                send_sem=sends.at[which],
                recv_sem=recvs.at[which],
                device_id=device,
                device_id_type=MESH,
            )
            for which in range(2)
        ]

    def right_copy(u, j):
        return pair(
            (kq.at[j, u], ks.at[j, u]),
            (lq.at[j, u], ls.at[j, u]),
            r_send.at[j, u],
            l_recv.at[j, u],
            (lax.rem(me_grid + 1, grid_size), me_basis),
        )

    def left_copy(u, j):
        return pair(
            (kq.at[j, u], ks.at[j, u]),
            (rq.at[j, u], rs.at[j, u]),
            r_send.at[j, u],
            r_recv.at[j, u],
            (lax.rem(me_grid + grid_size - 1, grid_size), me_basis),
        )

    def x_copy(u, d):
        to = lax.rem(me_basis + d, basis_size)
        its = lax.rem(to, members)
        return pair(
            (sq.at[u, its], ss.at[u, its]),
            (xq.at[d - 1, u], xs.at[d - 1, u]),
            x_send.at[d - 1, u],
            x_recv.at[d - 1, u],
            (me_grid, to),
        )

    def w_place(q):
        at = CL * q + me_grid * per
        return at // per_owner, lax.rem(at, per_owner) // per

    def w_copy(u, q):
        to, slot = w_place(q)
        return pair(
            (hq.at[q, u], hs.at[q, u]),
            (wq.at[slot, u], ws.at[slot, u]),
            w_send.at[q, u],
            w_recv.at[slot, u],
            (to, me_basis),
        )

    def w_arrival(u, slot):
        return pair(
            (hq.at[slot, u], hs.at[slot, u]),
            (wq.at[slot, u], ws.at[slot, u]),
            w_send.at[slot, u],
            w_recv.at[slot, u],
            (lax.rem(me_grid + 1, grid_size), me_basis),
        )

    def w_from(slot):
        return lax.rem(me_grid * per_owner + slot * per, CL) // per

    def partial_sum(u, j, m, i):
        return acc[j * per + u // halves, m * owned + u % halves * width + i]

    def pass_on(u, j, incoming):
        for m in range(members):
            for i in range(width):
                n = m * width + i
                total = partial_sum(u, j, m, i)
                if incoming is not None:
                    total += decode(incoming[0][j, u, n], incoming[1][j, u, pl.ds(n, 1), :])
                kq[j, u, n], ks[j, u, pl.ds(n, 1), :] = encode(total)

    def flow(u, e):
        @pl.when(me_grid + e < grid_size)
        def _():
            j = me_grid + e

            @pl.when(me_grid == 0)
            def _():
                pass_on(u, j, None)

            @pl.when(me_grid > 0)
            def _():
                for copy in right_copy(u, j):
                    copy.wait_recv()
                pass_on(u, j, (lq, ls))

            for copy in right_copy(u, j):
                copy.start()

        @pl.when(me_grid - e >= 0)
        def _():
            j = me_grid - e

            @pl.when(me_grid == grid_size - 1)
            def _():
                pass_on(u, j, None)

            @pl.when(me_grid < grid_size - 1)
            def _():
                for copy in left_copy(u, j):
                    copy.wait_recv()
                pass_on(u, j, (rq, rs))

            for copy in left_copy(u, j):
                copy.start()

    def settle(u):
        @pl.when(me_grid > 0)
        def _():
            for copy in right_copy(u, me_grid):
                copy.wait_recv()

        @pl.when(me_grid < grid_size - 1)
        def _():
            for copy in left_copy(u, me_grid):
                copy.wait_recv()

        def finish(sides):
            for m in range(members):
                for i in range(width):
                    n = m * width + i
                    total = partial_sum(u, me_grid, m, i)
                    for q, s in sides:
                        total += decode(q[me_grid, u, n], s[me_grid, u, pl.ds(n, 1), :])
                    sq[u, m, i], ss[u, m, pl.ds(i, 1), :] = encode(total.T)

        if grid_size == 1:
            finish([])
        else:

            @pl.when(me_grid == 0)
            def _():
                finish([(rq, rs)])

            @pl.when(me_grid == grid_size - 1)
            def _():
                finish([(lq, ls)])

            @pl.when((me_grid > 0) & (me_grid < grid_size - 1))
            def _():
                finish([(lq, ls), (rq, rs)])

        for d in range(1, basis_size):
            for copy in x_copy(u, d):
                copy.start()

    def wrap(number):
        return jnp.where(number < 0, number + block_count, number)

    def place(u):
        for d in range(1, basis_size):
            for copy in x_copy(u, d):
                copy.wait_recv()
        residue = me_grid * per + u // halves

        def spot(i, carry):
            block = me_basis * owned + u % halves * width + i
            totals = [None] * turns
            for d in range(basis_size):
                begin = firsts[d]
                inside = wrap(block - begin) < CL
                column = begin + ((residue - begin) & (CL - 1))
                column = jnp.where(column >= block_count, column - block_count, column)
                turn = column >> (CL.bit_length() - 1)
                if d == 0:
                    coded, scale = sq[u, mine, i], ss[u, mine, pl.ds(i, 1), :]
                else:
                    coded, scale = xq[d - 1, u, i], xs[d - 1, u, pl.ds(i, 1), :]
                number = coded.astype(jnp.int32).astype(jnp.float32)
                for q in range(turns):
                    term = number * jnp.where(inside & (turn == q), scale, 0.0)
                    totals[q] = term if totals[q] is None else totals[q] + term
            for q in range(turns):
                hq[q, u, i], hs[q, u, pl.ds(i, 1), :] = encode(totals[q])
            return carry

        lax.fori_loop(0, width, spot, 0)
        for q in range(turns):
            to, slot = w_place(q)

            @pl.when(to != me_grid)
            def _():
                for copy in w_copy(u, q):
                    copy.start()

            @pl.when(to == me_grid)
            def _():
                wq[slot, u] = hq[q, u]
                ws[slot, u] = hs[q, u]

    def deliver(u):
        for slot in range(turns):

            @pl.when(w_from(slot) != me_grid)
            def _():
                for copy in w_arrival(u, slot):
                    copy.wait_recv()

            column = (slot * per + u // halves) * TB
            for i in range(width):
                row = (u % halves * width + i) * TB
                out[row : row + TB, column : column + TB] = decode(
                    wq[slot, u, i], ws[slot, u, i : i + 1, :]
                )

    for u in range(units):
        for e in range(grid_size - 1, 0, -1):
            flow(u, e)
        settle(u)
        if u > 0:
            place(u - 1)
    place(units - 1)
    for u in range(units):
        deliver(u)

    for u in range(units):
        for e in range(1, grid_size):

            @pl.when(me_grid + e < grid_size)
            def _():
                for copy in right_copy(u, me_grid + e):
                    copy.wait_send()

            @pl.when(me_grid - e >= 0)
            def _():
                for copy in left_copy(u, me_grid - e):
                    copy.wait_send()

        for d in range(1, basis_size):
            for copy in x_copy(u, d):
                copy.wait_send()
        for q in range(turns):

            @pl.when(w_place(q)[0] != me_grid)
            def _():
                for copy in w_copy(u, q):
                    copy.wait_send()


def collect(acc, firsts, grid_size, basis_size, owned, turns):
    per = CL // grid_size
    members = CL // owned
    halves = math.gcd(owned, 2)
    width = owned // halves
    units = per * halves
    tiles = members * width
    vmem = pl.BlockSpec(memory_space=pltpu.VMEM)

    def both(*lead):
        return [
            pltpu.VMEM(lead + (TB, TB), jnp.int16),
            pltpu.VMEM(lead + (TB,), jnp.float32),
        ]

    dma = pltpu.SemaphoreType.DMA
    return pl.pallas_call(
        functools.partial(collect_kernel, grid_size, basis_size, owned, turns, halves),
        out_shape=jax.ShapeDtypeStruct((owned * TB, turns * per * TB), jnp.float32),
        in_specs=[vmem] * 2,
        out_specs=vmem,
        scratch_shapes=both(grid_size, units, tiles) * 3
        + both(units, members, width)
        + both(basis_size - 1, units, width)
        + both(turns, units, width)
        + both(turns, units, width)
        + [dma((grid_size, units, 2))] * 3
        + [dma((basis_size - 1, units, 2))] * 2
        + [dma((turns, units, 2))] * 2,
        compiler_params=pltpu.CompilerParams(
            collective_id=0, has_side_effects=True, vmem_limit_bytes=40 * 1024 * 1024
        ),
        name="collect",
    )(acc, firsts)


def body(
    basis_values,
    weights,
    points,
    block_lists,
    counts,
    density,
    centers,
    block_centers,
    block_exponents,
):
    basis_size = lax.axis_size("basis")
    grid_size = lax.axis_size("grid")
    block_count = block_exponents.shape[0]
    owned = block_count // basis_size
    turns = block_count // CL
    dens, coup, boys, weighted, firsts = prepare(
        basis_values, weights, points, block_lists, counts, density, centers, block_centers,
        block_exponents, grid_size, basis_size, owned,
    )
    acc = region_exchange(
        block_lists, counts, basis_values, weighted, boys, dens, coup, grid_size
    )
    return collect(acc, firsts, grid_size, basis_size, owned, turns)


def solution(mesh):
    placed = (
        P(("grid", "basis"), None, None),
        P(("grid", "basis"), None),
        P(("grid", "basis"), None, None),
        P(("grid", "basis"), None),
        P("basis", "grid"),
        P("basis", None),
        P(),
        P(),
        P(),
    )
    return jax.shard_map(
        body, mesh=mesh, in_specs=placed, out_specs=P("basis", "grid"), check_vma=False
    )
```

```python
import functools
import math

import jax
import jax.numpy as jnp
from jax import lax
from jax.experimental import pallas as pl
from jax.experimental.pallas import tpu as pltpu
from jax.sharding import PartitionSpec as P

TB = 128
CL = 8
PLACE_LAG = 1
DELIVER_LAG = 2
MESH = pl.DeviceIdType.MESH


def greet(me_grid, me_basis, grid_size, basis_size):
    barrier = pltpu.get_barrier_semaphore()
    for d in range(1, grid_size):
        pl.semaphore_signal(
            barrier,
            inc=1,
            device_id=(lax.rem(me_grid + d, grid_size), me_basis),
            device_id_type=MESH,
        )
    for d in range(1, basis_size):
        pl.semaphore_signal(
            barrier,
            inc=1,
            device_id=(me_grid, lax.rem(me_basis + d, basis_size)),
            device_id_type=MESH,
        )


def greeted(grid_size, basis_size):
    pl.semaphore_wait(pltpu.get_barrier_semaphore(), grid_size + basis_size - 2)


def encode(tile):
    top = jnp.maximum(jnp.max(jnp.abs(tile), axis=0, keepdims=True), 1e-30)
    steps = jnp.round(tile * (32767.0 / top))
    return steps.astype(jnp.int32).astype(jnp.int16), top * (1.0 / 32767.0)


def decode(coded, scale):
    return coded.astype(jnp.int32).astype(jnp.float32) * scale


def exchange_kernel(
    grid_size,
    basis_size,
    owned,
    turns,
    parts,
    group,
    lists_hbm,
    count_hbm,
    bc_hbm,
    be_hbm,
    weights_hbm,
    points_hbm,
    centers_hbm,
    values_hbm,
    density_hbm,
    out,
    values_v,
    density_v,
    packed,
    dens,
    coup,
    boys,
    wx,
    pots,
    potx,
    acc,
    firsts,
    first_v,
    firsts_s,
    wcol,
    cols,
    places,
    lists_ref,
    count_ref,
    bc_ref,
    be_ref,
    weights_ref,
    points_ref,
    centers_ref,
    kq,
    ks,
    lq,
    ls,
    rq,
    rs,
    sq,
    ss,
    xq,
    xs,
    hq,
    hs,
    wq,
    ws,
    small_sems,
    local_sem,
    d_sems,
    v_sems,
    f_send,
    f_recv,
    fx_send,
    fx_recv,
    fz_send,
    fz_recv,
    r_send,
    l_recv,
    r_recv,
    x_send,
    x_recv,
    w_send,
    w_recv,
    *landed,
):
    per = CL // grid_size
    rows = TB // parts
    chunks = per * parts
    lists, batches = lists_ref.shape
    block_count = be_ref.shape[0]
    point_total = weights_ref.shape[1]
    me_grid = lax.axis_index("grid")
    me_basis = lax.axis_index("basis")
    members_total = CL // owned
    per_owner = turns * per
    width = per
    units = owned
    mine = lax.rem(me_basis, members_total)

    greet(me_grid, me_basis, grid_size, basis_size)
    sources = (lists_hbm, count_hbm, bc_hbm, be_hbm, weights_hbm, points_hbm, centers_hbm)
    targets = (lists_ref, count_ref, bc_ref, be_ref, weights_ref, points_ref, centers_ref)
    small_in = [
        pltpu.make_async_copy(source, target, small_sems.at[n])
        for n, (source, target) in enumerate(zip(sources, targets))
    ]
    for copy in small_in:
        copy.start()

    def density_in(c):
        return pltpu.make_async_copy(
            density_hbm.at[:, c * TB : (c + 1) * TB], density_v.at[c], d_sems.at[c]
        )

    for c in range(block_count):
        density_in(c).start()

    def values_in(t):
        return pltpu.make_async_copy(
            values_hbm.at[:, :, t * TB : (t + 1) * TB], values_v.at[:, t], v_sems.at[t]
        )

    for t in range(lists):
        values_in(t).start()
    for copy in small_in:
        copy.wait()
    for c in range(block_count):
        places[c] = centers_ref[:, c * TB : (c + 1) * TB]

    half = block_count // 2
    origin = lists_ref[0, 0]
    low = jnp.int32(0)
    for b in range(batches):
        for t in range(lists):
            shift = lax.rem(lists_ref[t, b] - origin + block_count + half, block_count) - half
            low = jnp.minimum(low, shift)
    first = lax.rem(origin + low + block_count, block_count)
    first_v[...] = jnp.full(first_v.shape, first, jnp.int32)
    firsts[0] = jnp.full(firsts.shape[1:], first, jnp.int32)

    def member(begin, residue):
        return lax.rem(begin + ((residue - begin) & (CL - 1)), block_count)

    greeted(grid_size, basis_size)

    def f_copy(d):
        return pltpu.make_async_remote_copy(
            src_ref=first_v,
            dst_ref=firsts.at[d],
            send_sem=f_send.at[d - 1],
            recv_sem=f_recv.at[d - 1],
            device_id=(me_grid, lax.rem(me_basis + d, basis_size)),
            device_id_type=MESH,
        )

    for d in range(1, basis_size):
        f_copy(d).start()

    members = [member(first, r) for r in range(CL)]
    stacked = jnp.concatenate(
        [places[m] for m in members] + [jnp.zeros((TB - 3 * CL, TB), jnp.float32)], axis=0
    )
    cols[...] = stacked.T
    live = lax.broadcasted_iota(jnp.int32, weights_ref.shape, 0) < count_ref[0, 0]
    scaled = jnp.where(live, weights_ref[...], 0.0) / point_total
    scaled = jnp.concatenate(
        [scaled, jnp.zeros((TB - batches, point_total), jnp.float32)], axis=0
    )
    wcol[...] = scaled.T

    for d in range(1, basis_size):
        f_copy(d).wait_recv()
    firsts_in = pltpu.make_async_copy(firsts, firsts_s, local_sem)
    firsts_in.start()
    for c in range(block_count):
        density_in(c).wait()
    firsts_in.wait()

    def fx_copy(k, d):
        return pltpu.make_async_remote_copy(
            src_ref=packed.at[d, k],
            dst_ref=landed[k].at[d],
            send_sem=fx_send.at[d - 1, k],
            recv_sem=fx_recv.at[d - 1, k],
            device_id=(me_grid, lax.rem(me_basis + d, basis_size)),
            device_id_type=MESH,
        )

    def fz_copy(k, j, side):
        cc, part = k // parts, k % parts
        at = (j, cc, slice(None), pl.ds(part * rows, rows))
        return pltpu.make_async_remote_copy(
            src_ref=dens.at[at],
            dst_ref=dens.at[at],
            send_sem=fz_send.at[j, k, side],
            recv_sem=fz_recv.at[j, k],
            device_id=(me_grid + 1 if side == 0 else me_grid - 1, me_basis),
            device_id_type=MESH,
        )

    def pack(k, d):
        cc, part = k // parts, k % parts
        begin = firsts_s[lax.rem(basis_size - d, basis_size), 0, 0]
        if d == 0:
            column = member(first, me_grid * per + cc)
        else:
            column = member(begin, me_grid * per + cc)
        for i in range(owned):
            block = density_v[column, i * TB + part * rows : i * TB + (part + 1) * rows, :]
            if d == 0:
                landed[k][0, i] = block
            else:
                packed[d, k, i] = block

    slots = [lax.rem(me_basis - m // owned + basis_size, basis_size) for m in members]

    def own(k):
        cc, part = k // parts, k % parts
        for d in range(1, basis_size):
            fx_copy(k, d).wait_recv()
        for r in range(CL):
            dens[me_grid, cc, r, part * rows : (part + 1) * rows, :] = landed[k][
                slots[r], r % owned
            ]

        @pl.when(me_grid < grid_size - 1)
        def _():
            fz_copy(k, me_grid, 0).start()

        @pl.when(me_grid > 0)
        def _():
            fz_copy(k, me_grid, 1).start()

    def relay(k, h):
        @pl.when(me_grid >= h)
        def _():
            fz_copy(k, me_grid - h, 0).wait_recv()

            @pl.when(me_grid < grid_size - 1)
            def _():
                fz_copy(k, me_grid - h, 0).start()

        @pl.when(me_grid + h < grid_size)
        def _():
            fz_copy(k, me_grid + h, 1).wait_recv()

            @pl.when(me_grid > 0)
            def _():
                fz_copy(k, me_grid + h, 1).start()

    sharpness = float(centers_ref.shape[1]) ** (2.0 / 3.0)

    def couple(r):
        mine = [cols[:, 3 * r + d : 3 * r + d + 1] for d in range(3)]
        for u in range(CL):
            other = places[members[u]]
            spread = [mine[d] - other[d : d + 1] for d in range(3)]
            distance = spread[0] * spread[0] + spread[1] * spread[1] + spread[2] * spread[2]
            coup[r, u] = jnp.exp(-sharpness * distance).astype(jnp.bfloat16)

    pair_shape = (lists * lists, point_total)
    t_at = lax.broadcasted_iota(jnp.int32, pair_shape, 0) // lists
    u_at = lax.broadcasted_iota(jnp.int32, pair_shape, 0) % lists

    def positions(b):
        slots_at = [lists_ref[t, b] & (CL - 1) for t in range(lists)]
        spots = []
        for r in range(CL):
            spot = jnp.int32(lists)
            for t in range(lists):
                spot = jnp.where(slots_at[t] == r, t, spot)
            spots.append(spot)
        return spots

    def weigh(b):
        spots = positions(b)
        for r in range(CL):
            wx[b * point_total : (b + 1) * point_total, r * TB : (r + 1) * TB] = (
                values_v[b, spots[r]].astype(jnp.float32) * wcol[:, b : b + 1]
            ).astype(jnp.bfloat16)
        blocks = [lists_ref[t, b] for t in range(lists)]

        def spread_out(numbers, at):
            result = jnp.full(pair_shape, numbers[0], jnp.float32)
            for t in range(1, lists):
                result = jnp.where(at == t, numbers[t], result)
            return result

        distance = None
        for d in range(3):
            numbers = [bc_ref[d, block] for block in blocks]
            middle = 0.5 * (spread_out(numbers, t_at) + spread_out(numbers, u_at))
            offset = points_ref[d, b : b + 1, :].astype(jnp.float32) - middle
            square = offset * offset
            distance = square if distance is None else distance + square
        numbers = [be_ref[block] for block in blocks]
        rate = 0.5 * (spread_out(numbers, t_at) + spread_out(numbers, u_at))
        tau = rate * distance + 0.05
        root = jnp.sqrt(tau)
        boys[b] = 0.5 * math.sqrt(math.pi) * lax.erf(root) / root

    work = [functools.partial(couple, r) for r in range(CL)]
    work += [functools.partial(weigh, b) for b in range(batches)]
    share = -(-len(work) // chunks)

    for k in range(chunks):
        for d in range(1, basis_size):
            pack(k, d)
            fx_copy(k, d).start()
    for k in range(chunks):
        pack(k, 0)
    for t in range(lists):
        values_in(t).wait()
    values_v[:, lists] = jnp.zeros((batches, point_total, TB), jnp.bfloat16)
    for k in range(chunks + grid_size):
        for piece in work[k * share : (k + 1) * share]:
            piece()
        if k < chunks:
            own(k)
        for h in range(1, grid_size):
            if 0 <= k - h < chunks:
                relay(k - h, h)

    for g in range(group):
        pots[g, lists] = jnp.zeros((TB, point_total), jnp.bfloat16)

    def potential(n, carry):
        for g in range(group):
            b = n * group + g
            at = [lists_ref[t, b] & (CL - 1) for t in range(lists)]
            tiles = jnp.concatenate(
                [
                    jnp.concatenate([dens[c // per, lax.rem(c, per), r] for c in at], axis=1)
                    for r in at
                ],
                axis=0,
            )
            listed = jnp.concatenate([values_v[b, t] for t in range(lists)], axis=1)
            mapped = lax.dot_general(
                tiles, listed, (((1,), (1,)), ((), ())), preferred_element_type=jnp.float32
            ).astype(jnp.bfloat16)
            total = None
            for u in range(lists):
                side = jnp.concatenate([coup[r, at[u]] for r in at], axis=0)
                part = jnp.dot(
                    side, mapped[u * TB : (u + 1) * TB], preferred_element_type=jnp.float32
                )
                part = jnp.concatenate(
                    [
                        part[t * TB : (t + 1) * TB] * boys[b, t * lists + u : t * lists + u + 1, :]
                        for t in range(lists)
                    ],
                    axis=0,
                )
                total = part if total is None else total + part
            total = total.astype(jnp.bfloat16)
            for t in range(lists):
                pots[g, t] = total[t * TB : (t + 1) * TB]
            spots = positions(b)
            span = pl.ds(pl.multiple_of(b * point_total, point_total), point_total)
            for c in range(CL):
                potx[c * TB : (c + 1) * TB, span] = pots[g, spots[c]]
        return carry

    lax.fori_loop(0, batches // group, potential, 0)

    def sum_up(u):
        side = jnp.concatenate(
            [
                wx[:, (m * owned + u) * TB : (m * owned + u + 1) * TB]
                for m in range(members_total)
            ],
            axis=1,
        )
        total = jnp.dot(potx[...], side, preferred_element_type=jnp.float32)
        for c in range(CL):
            for m in range(members_total):
                acc[u, c, m] = total[c * TB : (c + 1) * TB, m * TB : (m + 1) * TB]

    def pair(sources, targets, sends, recvs, device):
        return [
            pltpu.make_async_remote_copy(
                src_ref=sources[which],
                dst_ref=targets[which],
                send_sem=sends.at[which],
                recv_sem=recvs.at[which],
                device_id=device,
                device_id_type=MESH,
            )
            for which in range(2)
        ]

    def right_copy(u, j):
        return pair(
            (kq.at[j, u], ks.at[j, u]),
            (lq.at[j, u], ls.at[j, u]),
            r_send.at[j, u],
            l_recv.at[j, u],
            (lax.rem(me_grid + 1, grid_size), me_basis),
        )

    def left_copy(u, j):
        return pair(
            (kq.at[j, u], ks.at[j, u]),
            (rq.at[j, u], rs.at[j, u]),
            r_send.at[j, u],
            r_recv.at[j, u],
            (lax.rem(me_grid + grid_size - 1, grid_size), me_basis),
        )

    def x_copy(u, d):
        to = lax.rem(me_basis + d, basis_size)
        its = lax.rem(to, members_total)
        return pair(
            (sq.at[u, its], ss.at[u, its]),
            (xq.at[d - 1, u], xs.at[d - 1, u]),
            x_send.at[d - 1, u],
            x_recv.at[d - 1, u],
            (me_grid, to),
        )

    def w_place(q):
        at = CL * q + me_grid * per
        return at // per_owner, lax.rem(at, per_owner) // per

    def w_copy(u, q):
        to, slot = w_place(q)
        return pair(
            (hq.at[q, u], hs.at[q, u]),
            (wq.at[slot, u], ws.at[slot, u]),
            w_send.at[q, u],
            w_recv.at[slot, u],
            (to, me_basis),
        )

    def w_arrival(u, slot):
        return pair(
            (hq.at[slot, u], hs.at[slot, u]),
            (wq.at[slot, u], ws.at[slot, u]),
            w_send.at[slot, u],
            w_recv.at[slot, u],
            (lax.rem(me_grid + 1, grid_size), me_basis),
        )

    def w_from(slot):
        return lax.rem(me_grid * per_owner + slot * per, CL) // per

    def partial_sum(u, j, m, i):
        return acc[u, j * per + i, m]

    def pass_on(u, j, incoming):
        for m in range(members_total):
            for i in range(width):
                n = m * width + i
                total = partial_sum(u, j, m, i)
                if incoming is not None:
                    total += decode(incoming[0][j, u, n], incoming[1][j, u, pl.ds(n, 1), :])
                kq[j, u, n], ks[j, u, pl.ds(n, 1), :] = encode(total)

    def flow(u, e):
        @pl.when(me_grid + e < grid_size)
        def _():
            j = me_grid + e

            @pl.when(me_grid == 0)
            def _():
                pass_on(u, j, None)

            @pl.when(me_grid > 0)
            def _():
                for copy in right_copy(u, j):
                    copy.wait_recv()
                pass_on(u, j, (lq, ls))

            for copy in right_copy(u, j):
                copy.start()

        @pl.when(me_grid - e >= 0)
        def _():
            j = me_grid - e

            @pl.when(me_grid == grid_size - 1)
            def _():
                pass_on(u, j, None)

            @pl.when(me_grid < grid_size - 1)
            def _():
                for copy in left_copy(u, j):
                    copy.wait_recv()
                pass_on(u, j, (rq, rs))

            for copy in left_copy(u, j):
                copy.start()

    def settle(u):
        @pl.when(me_grid > 0)
        def _():
            for copy in right_copy(u, me_grid):
                copy.wait_recv()

        @pl.when(me_grid < grid_size - 1)
        def _():
            for copy in left_copy(u, me_grid):
                copy.wait_recv()

        def finish(sides):
            for m in range(members_total):
                for i in range(width):
                    n = m * width + i
                    total = partial_sum(u, me_grid, m, i)
                    for q, s in sides:
                        total += decode(q[me_grid, u, n], s[me_grid, u, pl.ds(n, 1), :])
                    sq[u, m, i], ss[u, m, pl.ds(i, 1), :] = encode(total.T)

        if grid_size == 1:
            finish([])
        else:

            @pl.when(me_grid == 0)
            def _():
                finish([(rq, rs)])

            @pl.when(me_grid == grid_size - 1)
            def _():
                finish([(lq, ls)])

            @pl.when((me_grid > 0) & (me_grid < grid_size - 1))
            def _():
                finish([(lq, ls), (rq, rs)])

        for d in range(1, basis_size):
            for copy in x_copy(u, d):
                copy.start()

    def wrap(number):
        return jnp.where(number < 0, number + block_count, number)

    def place(u):
        for d in range(1, basis_size):
            for copy in x_copy(u, d):
                copy.wait_recv()
        block = me_basis * owned + u

        def spot(i, carry):
            residue = me_grid * per + i
            totals = [None] * turns
            for d in range(basis_size):
                begin = firsts[d]
                inside = wrap(block - begin) < CL
                column = begin + ((residue - begin) & (CL - 1))
                column = jnp.where(column >= block_count, column - block_count, column)
                turn = column >> (CL.bit_length() - 1)
                if d == 0:
                    coded, scale = sq[u, mine, i], ss[u, mine, pl.ds(i, 1), :]
                else:
                    coded, scale = xq[d - 1, u, i], xs[d - 1, u, pl.ds(i, 1), :]
                number = coded.astype(jnp.int32).astype(jnp.float32)
                for q in range(turns):
                    term = number * jnp.where(inside & (turn == q), scale, 0.0)
                    totals[q] = term if totals[q] is None else totals[q] + term
            for q in range(turns):
                hq[q, u, i], hs[q, u, pl.ds(i, 1), :] = encode(totals[q])
            return carry

        lax.fori_loop(0, width, spot, 0)
        for q in range(turns):
            to, slot = w_place(q)

            @pl.when(to != me_grid)
            def _():
                for copy in w_copy(u, q):
                    copy.start()

            @pl.when(to == me_grid)
            def _():
                wq[slot, u] = hq[q, u]
                ws[slot, u] = hs[q, u]

    def deliver(u):
        for slot in range(turns):

            @pl.when(w_from(slot) != me_grid)
            def _():
                for copy in w_arrival(u, slot):
                    copy.wait_recv()

            row = u * TB
            for i in range(width):
                column = (slot * per + i) * TB
                out[row : row + TB, column : column + TB] = decode(
                    wq[slot, u, i], ws[slot, u, i : i + 1, :]
                )

    hops = grid_size - 1
    for s in range(units + hops + PLACE_LAG + DELIVER_LAG):
        if s < units:
            sum_up(s)
        for e in range(hops, 0, -1):
            if 0 <= s - (hops - e) < units:
                flow(s - (hops - e), e)
        if 0 <= s - hops < units:
            settle(s - hops)
        if 0 <= s - hops - PLACE_LAG < units:
            place(s - hops - PLACE_LAG)
        if 0 <= s - hops - PLACE_LAG - DELIVER_LAG < units:
            deliver(s - hops - PLACE_LAG - DELIVER_LAG)

    for u in range(units):
        for e in range(1, grid_size):

            @pl.when(me_grid + e < grid_size)
            def _():
                for copy in right_copy(u, me_grid + e):
                    copy.wait_send()

            @pl.when(me_grid - e >= 0)
            def _():
                for copy in left_copy(u, me_grid - e):
                    copy.wait_send()

        for d in range(1, basis_size):
            for copy in x_copy(u, d):
                copy.wait_send()
        for q in range(turns):

            @pl.when(w_place(q)[0] != me_grid)
            def _():
                for copy in w_copy(u, q):
                    copy.wait_send()

    for d in range(1, basis_size):
        f_copy(d).wait_send()
    for k in range(chunks):
        for d in range(1, basis_size):
            fx_copy(k, d).wait_send()
        for h in range(grid_size):

            @pl.when((me_grid >= h) & (me_grid < grid_size - 1))
            def _():
                fz_copy(k, me_grid - h, 0).wait_send()

            @pl.when((me_grid + h < grid_size) & (me_grid > 0))
            def _():
                fz_copy(k, me_grid + h, 1).wait_send()


def exchange(
    values, weights, points, block_lists, counts, density, centers, block_centers, block_exponents,
    grid_size, basis_size,
):
    per = CL // grid_size
    parts = 8 // per
    chunks = per * parts
    batches, point_total, listed = values.shape
    lists = block_lists.shape[1]
    block_count = block_exponents.shape[0]
    owned = block_count // basis_size
    turns = block_count // CL
    members = CL // owned
    group = math.gcd(batches, 2)
    f32, bf16, i32 = jnp.float32, jnp.bfloat16, jnp.int32
    hbm = pl.BlockSpec(memory_space=pltpu.HBM)
    dma = pltpu.SemaphoreType.DMA

    def both(*lead):
        return [pltpu.VMEM(lead + (TB, TB), jnp.int16), pltpu.VMEM(lead + (TB,), f32)]

    scratch = [
        pltpu.VMEM((batches, lists + 1, point_total, TB), bf16),
        pltpu.VMEM((block_count, density.shape[0], TB), bf16),
        pltpu.VMEM((basis_size, chunks, owned, TB // parts, TB), bf16),
        pltpu.VMEM((grid_size, per, CL, TB, TB), bf16),
        pltpu.VMEM((CL, CL, TB, TB), bf16),
        pltpu.VMEM((batches, lists * lists, point_total), f32),
        pltpu.VMEM((batches * point_total, CL * TB), bf16),
        pltpu.VMEM((group, lists + 1, TB, point_total), bf16),
        pltpu.VMEM((CL * TB, batches * point_total), bf16),
        pltpu.VMEM((owned, CL, members, TB, TB), f32),
        pltpu.VMEM((basis_size, 1, TB), i32),
        pltpu.VMEM((1, TB), i32),
        pltpu.SMEM((basis_size, 1, TB), i32),
        pltpu.VMEM((point_total, TB), f32),
        pltpu.VMEM((TB, TB), f32),
        pltpu.VMEM((block_count, 3, TB), f32),
        pltpu.SMEM((lists, batches), i32),
        pltpu.SMEM((1, 1), i32),
        pltpu.SMEM(block_centers.shape, f32),
        pltpu.SMEM(block_exponents.shape, f32),
        pltpu.VMEM(weights.shape, f32),
        pltpu.VMEM((3, batches, point_total), bf16),
        pltpu.VMEM(centers.shape, f32),
    ]
    scratch += both(grid_size, owned, members * per) * 3
    scratch += both(owned, members, per) + both(basis_size - 1, owned, per)
    scratch += both(turns, owned, per) * 2
    scratch += [dma((7,)), dma(()), dma((block_count,)), dma((lists,))]
    scratch += [dma((basis_size - 1,))] * 2 + [dma((basis_size - 1, chunks))] * 2
    scratch += [dma((grid_size, chunks, 2)), dma((grid_size, chunks))]
    scratch += [dma((grid_size, owned, 2))] * 3 + [dma((basis_size - 1, owned, 2))] * 2
    scratch += [dma((turns, owned, 2))] * 2
    scratch += [pltpu.VMEM((basis_size, owned, TB // parts, TB), bf16) for k in range(chunks)]
    return pl.pallas_call(
        functools.partial(
            exchange_kernel, grid_size, basis_size, owned, turns, parts, group
        ),
        out_shape=jax.ShapeDtypeStruct((owned * TB, turns * per * TB), f32),
        in_specs=[hbm] * 9,
        out_specs=pl.BlockSpec(memory_space=pltpu.VMEM),
        scratch_shapes=scratch,
        compiler_params=pltpu.CompilerParams(
            collective_id=0, has_side_effects=True, vmem_limit_bytes=58 * 1024 * 1024
        ),
        name="exchange",
    )(
        block_lists.T, counts, block_centers, block_exponents, weights,
        points.transpose(1, 0, 2), centers, values, density,
    )


def body(*arrays):
    return exchange(*arrays, lax.axis_size("grid"), lax.axis_size("basis"))


def solution(mesh):
    placed = (
        P(("grid", "basis"), None, None),
        P(("grid", "basis"), None),
        P(("grid", "basis"), None, None),
        P(("grid", "basis"), None),
        P("basis", "grid"),
        P("basis", None),
        P(),
        P(),
        P(),
    )
    return jax.shard_map(
        body, mesh=mesh, in_specs=placed, out_specs=P("basis", "grid"), check_vma=False
    )
```

```python
import functools
import math

import jax
import jax.numpy as jnp
from jax import lax
from jax.experimental import pallas as pl
from jax.experimental.pallas import tpu as pltpu
from jax.sharding import PartitionSpec as P

TB = 128
CL = 8
PLACE_LAG = 1
DELIVER_LAG = 2
MESH = pl.DeviceIdType.MESH


def greet(me_grid, me_basis, grid_size, basis_size):
    barrier = pltpu.get_barrier_semaphore()
    for d in range(1, grid_size):
        pl.semaphore_signal(
            barrier,
            inc=1,
            device_id=(lax.rem(me_grid + d, grid_size), me_basis),
            device_id_type=MESH,
        )
    for d in range(1, basis_size):
        pl.semaphore_signal(
            barrier,
            inc=1,
            device_id=(me_grid, lax.rem(me_basis + d, basis_size)),
            device_id_type=MESH,
        )


def greeted(grid_size, basis_size):
    pl.semaphore_wait(pltpu.get_barrier_semaphore(), grid_size + basis_size - 2)


def encode(tile):
    top = jnp.maximum(jnp.max(jnp.abs(tile), axis=0, keepdims=True), 1e-30)
    steps = jnp.round(tile * (32767.0 / top))
    return steps.astype(jnp.int32).astype(jnp.int16), top * (1.0 / 32767.0)


def decode(coded, scale):
    return coded.astype(jnp.int32).astype(jnp.float32) * scale


def exchange_kernel(
    grid_size,
    basis_size,
    owned,
    turns,
    parts,
    group,
    lists_hbm,
    count_hbm,
    bc_hbm,
    be_hbm,
    weights_hbm,
    points_hbm,
    centers_hbm,
    values_hbm,
    density_hbm,
    out_hbm,
    out,
    out_sems,
    values_v,
    density_v,
    packed,
    dens,
    coup,
    boys,
    wx,
    pots,
    potx,
    acc,
    firsts,
    first_v,
    firsts_s,
    wcol,
    cols,
    places,
    lists_ref,
    count_ref,
    bc_ref,
    be_ref,
    weights_ref,
    points_ref,
    centers_ref,
    kq,
    ks,
    lq,
    ls,
    rq,
    rs,
    sq,
    ss,
    xq,
    xs,
    hq,
    hs,
    wq,
    ws,
    small_sems,
    local_sem,
    d_sems,
    v_sems,
    f_send,
    f_recv,
    fx_send,
    fx_recv,
    fz_send,
    fz_recv,
    r_send,
    l_recv,
    r_recv,
    x_send,
    x_recv,
    w_send,
    w_recv,
    *landed,
):
    per = CL // grid_size
    rows = TB // parts
    chunks = per * parts
    lists, batches = lists_ref.shape
    block_count = be_ref.shape[0]
    point_total = weights_ref.shape[1]
    me_grid = lax.axis_index("grid")
    me_basis = lax.axis_index("basis")
    members_total = CL // owned
    per_owner = turns * per
    width = per
    units = owned
    mine = lax.rem(me_basis, members_total)

    greet(me_grid, me_basis, grid_size, basis_size)
    sources = (lists_hbm, count_hbm, bc_hbm, be_hbm, weights_hbm, points_hbm, centers_hbm)
    targets = (lists_ref, count_ref, bc_ref, be_ref, weights_ref, points_ref, centers_ref)
    small_in = [
        pltpu.make_async_copy(source, target, small_sems.at[n])
        for n, (source, target) in enumerate(zip(sources, targets))
    ]
    for copy in small_in:
        copy.start()

    def density_in(c):
        return pltpu.make_async_copy(
            density_hbm.at[:, c * TB : (c + 1) * TB], density_v.at[c], d_sems.at[c]
        )

    for c in range(block_count):
        density_in(c).start()

    def values_in(t):
        return pltpu.make_async_copy(
            values_hbm.at[:, :, t * TB : (t + 1) * TB], values_v.at[:, t], v_sems.at[t]
        )

    for t in range(lists):
        values_in(t).start()
    for copy in small_in:
        copy.wait()
    for c in range(block_count):
        places[c] = centers_ref[:, c * TB : (c + 1) * TB]

    half = block_count // 2
    origin = lists_ref[0, 0]
    low = jnp.int32(0)
    for b in range(batches):
        for t in range(lists):
            shift = lax.rem(lists_ref[t, b] - origin + block_count + half, block_count) - half
            low = jnp.minimum(low, shift)
    first = lax.rem(origin + low + block_count, block_count)
    first_v[...] = jnp.full(first_v.shape, first, jnp.int32)
    firsts[0] = jnp.full(firsts.shape[1:], first, jnp.int32)

    def member(begin, residue):
        return lax.rem(begin + ((residue - begin) & (CL - 1)), block_count)

    greeted(grid_size, basis_size)

    def f_copy(d):
        return pltpu.make_async_remote_copy(
            src_ref=first_v,
            dst_ref=firsts.at[d],
            send_sem=f_send.at[d - 1],
            recv_sem=f_recv.at[d - 1],
            device_id=(me_grid, lax.rem(me_basis + d, basis_size)),
            device_id_type=MESH,
        )

    for d in range(1, basis_size):
        f_copy(d).start()

    members = [member(first, r) for r in range(CL)]
    stacked = jnp.concatenate(
        [places[m] for m in members] + [jnp.zeros((TB - 3 * CL, TB), jnp.float32)], axis=0
    )
    cols[...] = stacked.T
    live = lax.broadcasted_iota(jnp.int32, weights_ref.shape, 0) < count_ref[0, 0]
    scaled = jnp.where(live, weights_ref[...], 0.0) / point_total
    scaled = jnp.concatenate(
        [scaled, jnp.zeros((TB - batches, point_total), jnp.float32)], axis=0
    )
    wcol[...] = scaled.T

    for d in range(1, basis_size):
        f_copy(d).wait_recv()
    firsts_in = pltpu.make_async_copy(firsts, firsts_s, local_sem)
    firsts_in.start()
    for c in range(block_count):
        density_in(c).wait()
    firsts_in.wait()

    def fx_copy(k, d):
        return pltpu.make_async_remote_copy(
            src_ref=packed.at[d, k],
            dst_ref=landed[k].at[d],
            send_sem=fx_send.at[d - 1, k],
            recv_sem=fx_recv.at[d - 1, k],
            device_id=(me_grid, lax.rem(me_basis + d, basis_size)),
            device_id_type=MESH,
        )

    def fz_copy(k, j, side):
        cc, part = k // parts, k % parts
        at = (j, cc, slice(None), pl.ds(part * rows, rows))
        return pltpu.make_async_remote_copy(
            src_ref=dens.at[at],
            dst_ref=dens.at[at],
            send_sem=fz_send.at[j, k, side],
            recv_sem=fz_recv.at[j, k],
            device_id=(me_grid + 1 if side == 0 else me_grid - 1, me_basis),
            device_id_type=MESH,
        )

    def pack(k, d):
        cc, part = k // parts, k % parts
        begin = firsts_s[lax.rem(basis_size - d, basis_size), 0, 0]
        if d == 0:
            column = member(first, me_grid * per + cc)
        else:
            column = member(begin, me_grid * per + cc)
        for i in range(owned):
            block = density_v[column, i * TB + part * rows : i * TB + (part + 1) * rows, :]
            if d == 0:
                landed[k][0, i] = block
            else:
                packed[d, k, i] = block

    slots = [lax.rem(me_basis - m // owned + basis_size, basis_size) for m in members]

    def own(k):
        cc, part = k // parts, k % parts
        for d in range(1, basis_size):
            fx_copy(k, d).wait_recv()
        for r in range(CL):
            dens[me_grid, cc, r, part * rows : (part + 1) * rows, :] = landed[k][
                slots[r], r % owned
            ]

        @pl.when(me_grid < grid_size - 1)
        def _():
            fz_copy(k, me_grid, 0).start()

        @pl.when(me_grid > 0)
        def _():
            fz_copy(k, me_grid, 1).start()

    def relay(k, h):
        @pl.when(me_grid >= h)
        def _():
            fz_copy(k, me_grid - h, 0).wait_recv()

            @pl.when(me_grid < grid_size - 1)
            def _():
                fz_copy(k, me_grid - h, 0).start()

        @pl.when(me_grid + h < grid_size)
        def _():
            fz_copy(k, me_grid + h, 1).wait_recv()

            @pl.when(me_grid > 0)
            def _():
                fz_copy(k, me_grid + h, 1).start()

    sharpness = float(centers_ref.shape[1]) ** (2.0 / 3.0)

    def couple(r):
        mine = [cols[:, 3 * r + d : 3 * r + d + 1] for d in range(3)]
        for u in range(CL):
            other = places[members[u]]
            spread = [mine[d] - other[d : d + 1] for d in range(3)]
            distance = spread[0] * spread[0] + spread[1] * spread[1] + spread[2] * spread[2]
            coup[r, u] = jnp.exp(-sharpness * distance).astype(jnp.bfloat16)

    pair_shape = (lists * lists, point_total)
    t_at = lax.broadcasted_iota(jnp.int32, pair_shape, 0) // lists
    u_at = lax.broadcasted_iota(jnp.int32, pair_shape, 0) % lists

    def positions(b):
        slots_at = [lists_ref[t, b] & (CL - 1) for t in range(lists)]
        spots = []
        for r in range(CL):
            spot = jnp.int32(lists)
            for t in range(lists):
                spot = jnp.where(slots_at[t] == r, t, spot)
            spots.append(spot)
        return spots

    def weigh(b):
        spots = positions(b)
        for r in range(CL):
            wx[b * point_total : (b + 1) * point_total, r * TB : (r + 1) * TB] = (
                values_v[b, spots[r]].astype(jnp.float32) * wcol[:, b : b + 1]
            ).astype(jnp.bfloat16)
        blocks = [lists_ref[t, b] for t in range(lists)]

        def spread_out(numbers, at):
            result = jnp.full(pair_shape, numbers[0], jnp.float32)
            for t in range(1, lists):
                result = jnp.where(at == t, numbers[t], result)
            return result

        distance = None
        for d in range(3):
            numbers = [bc_ref[d, block] for block in blocks]
            middle = 0.5 * (spread_out(numbers, t_at) + spread_out(numbers, u_at))
            offset = points_ref[d, b : b + 1, :].astype(jnp.float32) - middle
            square = offset * offset
            distance = square if distance is None else distance + square
        numbers = [be_ref[block] for block in blocks]
        rate = 0.5 * (spread_out(numbers, t_at) + spread_out(numbers, u_at))
        tau = rate * distance + 0.05
        root = jnp.sqrt(tau)
        boys[b] = 0.5 * math.sqrt(math.pi) * lax.erf(root) / root

    work = [functools.partial(couple, r) for r in range(CL)]
    work += [functools.partial(weigh, b) for b in range(batches)]
    share = -(-len(work) // chunks)

    for k in range(chunks):
        for d in range(1, basis_size):
            pack(k, d)
            fx_copy(k, d).start()
    for k in range(chunks):
        pack(k, 0)
    for t in range(lists):
        values_in(t).wait()
    values_v[:, lists] = jnp.zeros((batches, point_total, TB), jnp.bfloat16)
    for k in range(chunks + grid_size):
        for piece in work[k * share : (k + 1) * share]:
            piece()
        if k < chunks:
            own(k)
        for h in range(1, grid_size):
            if 0 <= k - h < chunks:
                relay(k - h, h)

    for g in range(group):
        pots[g, lists] = jnp.zeros((TB, point_total), jnp.bfloat16)

    def potential(n, carry):
        for g in range(group):
            b = n * group + g
            at = [lists_ref[t, b] & (CL - 1) for t in range(lists)]
            tiles = jnp.concatenate(
                [
                    jnp.concatenate([dens[c // per, lax.rem(c, per), r] for c in at], axis=1)
                    for r in at
                ],
                axis=0,
            )
            listed = jnp.concatenate([values_v[b, t] for t in range(lists)], axis=1)
            mapped = lax.dot_general(
                tiles, listed, (((1,), (1,)), ((), ())), preferred_element_type=jnp.float32
            ).astype(jnp.bfloat16)
            total = None
            for u in range(lists):
                side = jnp.concatenate([coup[r, at[u]] for r in at], axis=0)
                part = jnp.dot(
                    side, mapped[u * TB : (u + 1) * TB], preferred_element_type=jnp.float32
                )
                part = jnp.concatenate(
                    [
                        part[t * TB : (t + 1) * TB] * boys[b, t * lists + u : t * lists + u + 1, :]
                        for t in range(lists)
                    ],
                    axis=0,
                )
                total = part if total is None else total + part
            total = total.astype(jnp.bfloat16)
            for t in range(lists):
                pots[g, t] = total[t * TB : (t + 1) * TB]
            spots = positions(b)
            span = pl.ds(pl.multiple_of(b * point_total, point_total), point_total)
            for c in range(CL):
                potx[c * TB : (c + 1) * TB, span] = pots[g, spots[c]]
        return carry

    lax.fori_loop(0, batches // group, potential, 0)

    def sum_up(u):
        side = jnp.concatenate(
            [
                wx[:, (m * owned + u) * TB : (m * owned + u + 1) * TB]
                for m in range(members_total)
            ],
            axis=1,
        )
        total = jnp.dot(potx[...], side, preferred_element_type=jnp.float32)
        for c in range(CL):
            for m in range(members_total):
                acc[u, c, m] = total[c * TB : (c + 1) * TB, m * TB : (m + 1) * TB]

    def pair(sources, targets, sends, recvs, device):
        return [
            pltpu.make_async_remote_copy(
                src_ref=sources[which],
                dst_ref=targets[which],
                send_sem=sends.at[which],
                recv_sem=recvs.at[which],
                device_id=device,
                device_id_type=MESH,
            )
            for which in range(2)
        ]

    def right_copy(u, j):
        return pair(
            (kq.at[j, u], ks.at[j, u]),
            (lq.at[j, u], ls.at[j, u]),
            r_send.at[j, u],
            l_recv.at[j, u],
            (lax.rem(me_grid + 1, grid_size), me_basis),
        )

    def left_copy(u, j):
        return pair(
            (kq.at[j, u], ks.at[j, u]),
            (rq.at[j, u], rs.at[j, u]),
            r_send.at[j, u],
            r_recv.at[j, u],
            (lax.rem(me_grid + grid_size - 1, grid_size), me_basis),
        )

    def x_copy(u, d):
        to = lax.rem(me_basis + d, basis_size)
        its = lax.rem(to, members_total)
        return pair(
            (sq.at[u, its], ss.at[u, its]),
            (xq.at[d - 1, u], xs.at[d - 1, u]),
            x_send.at[d - 1, u],
            x_recv.at[d - 1, u],
            (me_grid, to),
        )

    def w_place(q):
        at = CL * q + me_grid * per
        return at // per_owner, lax.rem(at, per_owner) // per

    def w_copy(u, q):
        to, slot = w_place(q)
        return pair(
            (hq.at[q, u], hs.at[q, u]),
            (wq.at[slot, u], ws.at[slot, u]),
            w_send.at[q, u],
            w_recv.at[slot, u],
            (to, me_basis),
        )

    def w_arrival(u, slot):
        return pair(
            (hq.at[slot, u], hs.at[slot, u]),
            (wq.at[slot, u], ws.at[slot, u]),
            w_send.at[slot, u],
            w_recv.at[slot, u],
            (lax.rem(me_grid + 1, grid_size), me_basis),
        )

    def w_from(slot):
        return lax.rem(me_grid * per_owner + slot * per, CL) // per

    def partial_sum(u, j, m, i):
        return acc[u, j * per + i, m]

    def pass_on(u, j, incoming):
        for m in range(members_total):
            for i in range(width):
                n = m * width + i
                total = partial_sum(u, j, m, i)
                if incoming is not None:
                    total += decode(incoming[0][j, u, n], incoming[1][j, u, pl.ds(n, 1), :])
                kq[j, u, n], ks[j, u, pl.ds(n, 1), :] = encode(total)

    def flow(u, e):
        @pl.when(me_grid + e < grid_size)
        def _():
            j = me_grid + e

            @pl.when(me_grid == 0)
            def _():
                pass_on(u, j, None)

            @pl.when(me_grid > 0)
            def _():
                for copy in right_copy(u, j):
                    copy.wait_recv()
                pass_on(u, j, (lq, ls))

            for copy in right_copy(u, j):
                copy.start()

        @pl.when(me_grid - e >= 0)
        def _():
            j = me_grid - e

            @pl.when(me_grid == grid_size - 1)
            def _():
                pass_on(u, j, None)

            @pl.when(me_grid < grid_size - 1)
            def _():
                for copy in left_copy(u, j):
                    copy.wait_recv()
                pass_on(u, j, (rq, rs))

            for copy in left_copy(u, j):
                copy.start()

    def settle(u):
        @pl.when(me_grid > 0)
        def _():
            for copy in right_copy(u, me_grid):
                copy.wait_recv()

        @pl.when(me_grid < grid_size - 1)
        def _():
            for copy in left_copy(u, me_grid):
                copy.wait_recv()

        def finish(sides):
            for m in range(members_total):
                for i in range(width):
                    n = m * width + i
                    total = partial_sum(u, me_grid, m, i)
                    for q, s in sides:
                        total += decode(q[me_grid, u, n], s[me_grid, u, pl.ds(n, 1), :])
                    sq[u, m, i], ss[u, m, pl.ds(i, 1), :] = encode(total.T)

        if grid_size == 1:
            finish([])
        else:

            @pl.when(me_grid == 0)
            def _():
                finish([(rq, rs)])

            @pl.when(me_grid == grid_size - 1)
            def _():
                finish([(lq, ls)])

            @pl.when((me_grid > 0) & (me_grid < grid_size - 1))
            def _():
                finish([(lq, ls), (rq, rs)])

        for d in range(1, basis_size):
            for copy in x_copy(u, d):
                copy.start()

    def wrap(number):
        return jnp.where(number < 0, number + block_count, number)

    def place(u):
        for d in range(1, basis_size):
            for copy in x_copy(u, d):
                copy.wait_recv()
        block = me_basis * owned + u

        def spot(i, carry):
            residue = me_grid * per + i
            totals = [None] * turns
            for d in range(basis_size):
                begin = firsts[d]
                inside = wrap(block - begin) < CL
                column = begin + ((residue - begin) & (CL - 1))
                column = jnp.where(column >= block_count, column - block_count, column)
                turn = column >> (CL.bit_length() - 1)
                if d == 0:
                    coded, scale = sq[u, mine, i], ss[u, mine, pl.ds(i, 1), :]
                else:
                    coded, scale = xq[d - 1, u, i], xs[d - 1, u, pl.ds(i, 1), :]
                number = coded.astype(jnp.int32).astype(jnp.float32)
                for q in range(turns):
                    term = number * jnp.where(inside & (turn == q), scale, 0.0)
                    totals[q] = term if totals[q] is None else totals[q] + term
            for q in range(turns):
                hq[q, u, i], hs[q, u, pl.ds(i, 1), :] = encode(totals[q])
            return carry

        lax.fori_loop(0, width, spot, 0)
        for q in range(turns):
            to, slot = w_place(q)

            @pl.when(to != me_grid)
            def _():
                for copy in w_copy(u, q):
                    copy.start()

            @pl.when(to == me_grid)
            def _():
                wq[slot, u] = hq[q, u]
                ws[slot, u] = hs[q, u]

    def out_copy(u):
        at = slice(u * TB, (u + 1) * TB)
        return pltpu.make_async_copy(out.at[at], out_hbm.at[at], out_sems.at[u])

    def deliver(u):
        for slot in range(turns):

            @pl.when(w_from(slot) != me_grid)
            def _():
                for copy in w_arrival(u, slot):
                    copy.wait_recv()

            row = u * TB
            for i in range(width):
                column = (slot * per + i) * TB
                out[row : row + TB, column : column + TB] = decode(
                    wq[slot, u, i], ws[slot, u, i : i + 1, :]
                )
        out_copy(u).start()

    hops = grid_size - 1
    for s in range(units + hops + PLACE_LAG + DELIVER_LAG):
        if s < units:
            sum_up(s)
        for e in range(hops, 0, -1):
            if 0 <= s - (hops - e) < units:
                flow(s - (hops - e), e)
        if 0 <= s - hops < units:
            settle(s - hops)
        if 0 <= s - hops - PLACE_LAG < units:
            place(s - hops - PLACE_LAG)
        if 0 <= s - hops - PLACE_LAG - DELIVER_LAG < units:
            deliver(s - hops - PLACE_LAG - DELIVER_LAG)

    for u in range(units):
        out_copy(u).wait()
        for e in range(1, grid_size):

            @pl.when(me_grid + e < grid_size)
            def _():
                for copy in right_copy(u, me_grid + e):
                    copy.wait_send()

            @pl.when(me_grid - e >= 0)
            def _():
                for copy in left_copy(u, me_grid - e):
                    copy.wait_send()

        for d in range(1, basis_size):
            for copy in x_copy(u, d):
                copy.wait_send()
        for q in range(turns):

            @pl.when(w_place(q)[0] != me_grid)
            def _():
                for copy in w_copy(u, q):
                    copy.wait_send()

    for d in range(1, basis_size):
        f_copy(d).wait_send()
    for k in range(chunks):
        for d in range(1, basis_size):
            fx_copy(k, d).wait_send()
        for h in range(grid_size):

            @pl.when((me_grid >= h) & (me_grid < grid_size - 1))
            def _():
                fz_copy(k, me_grid - h, 0).wait_send()

            @pl.when((me_grid + h < grid_size) & (me_grid > 0))
            def _():
                fz_copy(k, me_grid + h, 1).wait_send()


def exchange(
    values, weights, points, block_lists, counts, density, centers, block_centers, block_exponents,
    grid_size, basis_size,
):
    per = CL // grid_size
    parts = 8 // per
    chunks = per * parts
    batches, point_total, listed = values.shape
    lists = block_lists.shape[1]
    block_count = block_exponents.shape[0]
    owned = block_count // basis_size
    turns = block_count // CL
    members = CL // owned
    group = math.gcd(batches, 8)
    f32, bf16, i32 = jnp.float32, jnp.bfloat16, jnp.int32
    hbm = pl.BlockSpec(memory_space=pltpu.HBM)
    dma = pltpu.SemaphoreType.DMA

    def both(*lead):
        return [pltpu.VMEM(lead + (TB, TB), jnp.int16), pltpu.VMEM(lead + (TB,), f32)]

    scratch = [
        pltpu.VMEM((owned * TB, turns * per * TB), f32),
        dma((owned,)),
        pltpu.VMEM((batches, lists + 1, point_total, TB), bf16),
        pltpu.VMEM((block_count, density.shape[0], TB), bf16),
        pltpu.VMEM((basis_size, chunks, owned, TB // parts, TB), bf16),
        pltpu.VMEM((grid_size, per, CL, TB, TB), bf16),
        pltpu.VMEM((CL, CL, TB, TB), bf16),
        pltpu.VMEM((batches, lists * lists, point_total), f32),
        pltpu.VMEM((batches * point_total, CL * TB), bf16),
        pltpu.VMEM((group, lists + 1, TB, point_total), bf16),
        pltpu.VMEM((CL * TB, batches * point_total), bf16),
        pltpu.VMEM((owned, CL, members, TB, TB), f32),
        pltpu.VMEM((basis_size, 1, TB), i32),
        pltpu.VMEM((1, TB), i32),
        pltpu.SMEM((basis_size, 1, TB), i32),
        pltpu.VMEM((point_total, TB), f32),
        pltpu.VMEM((TB, TB), f32),
        pltpu.VMEM((block_count, 3, TB), f32),
        pltpu.SMEM((lists, batches), i32),
        pltpu.SMEM((1, 1), i32),
        pltpu.SMEM(block_centers.shape, f32),
        pltpu.SMEM(block_exponents.shape, f32),
        pltpu.VMEM(weights.shape, f32),
        pltpu.VMEM((3, batches, point_total), bf16),
        pltpu.VMEM(centers.shape, f32),
    ]
    scratch += both(grid_size, owned, members * per) * 3
    scratch += both(owned, members, per) + both(basis_size - 1, owned, per)
    scratch += both(turns, owned, per) * 2
    scratch += [dma((7,)), dma(()), dma((block_count,)), dma((lists,))]
    scratch += [dma((basis_size - 1,))] * 2 + [dma((basis_size - 1, chunks))] * 2
    scratch += [dma((grid_size, chunks, 2)), dma((grid_size, chunks))]
    scratch += [dma((grid_size, owned, 2))] * 3 + [dma((basis_size - 1, owned, 2))] * 2
    scratch += [dma((turns, owned, 2))] * 2
    scratch += [pltpu.VMEM((basis_size, owned, TB // parts, TB), bf16) for k in range(chunks)]
    return pl.pallas_call(
        functools.partial(
            exchange_kernel, grid_size, basis_size, owned, turns, parts, group
        ),
        out_shape=jax.ShapeDtypeStruct((owned * TB, turns * per * TB), f32),
        in_specs=[hbm] * 9,
        out_specs=hbm,
        scratch_shapes=scratch,
        compiler_params=pltpu.CompilerParams(
            collective_id=0, has_side_effects=True, vmem_limit_bytes=58 * 1024 * 1024
        ),
        name="exchange",
    )(
        block_lists.T, counts, block_centers, block_exponents, weights,
        points.transpose(1, 0, 2), centers, values, density,
    )


def body(*arrays):
    return exchange(*arrays, lax.axis_size("grid"), lax.axis_size("basis"))


def solution(mesh):
    placed = (
        P(("grid", "basis"), None, None),
        P(("grid", "basis"), None),
        P(("grid", "basis"), None, None),
        P(("grid", "basis"), None),
        P("basis", "grid"),
        P("basis", None),
        P(),
        P(),
        P(),
    )
    return jax.shard_map(
        body, mesh=mesh, in_specs=placed, out_specs=P("basis", "grid"), check_vma=False
    )
```

```python
import functools
import math

import jax
import jax.numpy as jnp
from jax import lax
from jax.experimental import pallas as pl
from jax.experimental.pallas import tpu as pltpu
from jax.sharding import PartitionSpec as P

TB = 128
CL = 8
PLACE_LAG = 1
DELIVER_LAG = 2
MESH = pl.DeviceIdType.MESH


def greet(me_grid, me_basis, grid_size, basis_size):
    barrier = pltpu.get_barrier_semaphore()
    for d in range(1, grid_size):
        pl.semaphore_signal(
            barrier,
            inc=1,
            device_id=(lax.rem(me_grid + d, grid_size), me_basis),
            device_id_type=MESH,
        )
    for d in range(1, basis_size):
        pl.semaphore_signal(
            barrier,
            inc=1,
            device_id=(me_grid, lax.rem(me_basis + d, basis_size)),
            device_id_type=MESH,
        )


def greeted(grid_size, basis_size):
    pl.semaphore_wait(pltpu.get_barrier_semaphore(), grid_size + basis_size - 2)


def encode(tile):
    top = jnp.maximum(jnp.max(jnp.abs(tile), axis=0, keepdims=True), 1e-30)
    steps = jnp.round(tile * (32767.0 / top))
    return steps.astype(jnp.int32).astype(jnp.int16), top * (1.0 / 32767.0)


def decode(coded, scale):
    return coded.astype(jnp.int32).astype(jnp.float32) * scale


def exchange_kernel(
    grid_size,
    basis_size,
    owned,
    turns,
    parts,
    group,
    lists_hbm,
    count_hbm,
    bc_hbm,
    be_hbm,
    weights_hbm,
    points_hbm,
    centers_hbm,
    values_hbm,
    density_hbm,
    out_hbm,
    out,
    out_sems,
    values_v,
    density_v,
    packed,
    dens,
    coup,
    boys,
    wx,
    pots,
    potx,
    acc,
    firsts,
    first_v,
    firsts_s,
    wcol,
    cols,
    places,
    lists_ref,
    count_ref,
    bc_ref,
    be_ref,
    weights_ref,
    points_ref,
    centers_ref,
    kq,
    ks,
    lq,
    ls,
    rq,
    rs,
    sq,
    ss,
    xq,
    xs,
    hq,
    hs,
    wq,
    ws,
    small_sems,
    local_sem,
    d_sems,
    v_sems,
    f_send,
    f_recv,
    fx_send,
    fx_recv,
    fz_send,
    fz_recv,
    r_send,
    l_recv,
    r_recv,
    x_send,
    x_recv,
    w_send,
    w_recv,
    *landed,
):
    per = CL // grid_size
    rows = TB // parts
    chunks = per * parts
    lists, batches = lists_ref.shape
    block_count = be_ref.shape[0]
    point_total = weights_ref.shape[1]
    me_grid = lax.axis_index("grid")
    me_basis = lax.axis_index("basis")
    members_total = CL // owned
    per_owner = turns * per
    width = per
    units = owned
    mine = lax.rem(me_basis, members_total)

    greet(me_grid, me_basis, grid_size, basis_size)
    sources = (lists_hbm, count_hbm, bc_hbm, be_hbm, weights_hbm, points_hbm, centers_hbm)
    targets = (lists_ref, count_ref, bc_ref, be_ref, weights_ref, points_ref, centers_ref)
    small_in = [
        pltpu.make_async_copy(source, target, small_sems.at[n])
        for n, (source, target) in enumerate(zip(sources, targets))
    ]
    for copy in small_in:
        copy.start()

    def density_in(c):
        return pltpu.make_async_copy(
            density_hbm.at[:, c * TB : (c + 1) * TB], density_v.at[c], d_sems.at[c]
        )

    for c in range(block_count):
        density_in(c).start()

    def values_in(t):
        return pltpu.make_async_copy(
            values_hbm.at[:, :, t * TB : (t + 1) * TB], values_v.at[:, t], v_sems.at[t]
        )

    for t in range(lists):
        values_in(t).start()
    for copy in small_in:
        copy.wait()
    for c in range(block_count):
        places[c] = centers_ref[:, c * TB : (c + 1) * TB]

    half = block_count // 2
    origin = lists_ref[0, 0]
    low = jnp.int32(0)
    for b in range(batches):
        for t in range(lists):
            shift = lax.rem(lists_ref[t, b] - origin + block_count + half, block_count) - half
            low = jnp.minimum(low, shift)
    first = lax.rem(origin + low + block_count, block_count)
    first_v[...] = jnp.full(first_v.shape, first, jnp.int32)
    firsts[0] = jnp.full(firsts.shape[1:], first, jnp.int32)

    def member(begin, residue):
        return lax.rem(begin + ((residue - begin) & (CL - 1)), block_count)

    greeted(grid_size, basis_size)

    def f_copy(d):
        return pltpu.make_async_remote_copy(
            src_ref=first_v,
            dst_ref=firsts.at[d],
            send_sem=f_send.at[d - 1],
            recv_sem=f_recv.at[d - 1],
            device_id=(me_grid, lax.rem(me_basis + d, basis_size)),
            device_id_type=MESH,
        )

    for d in range(1, basis_size):
        f_copy(d).start()

    members = [member(first, r) for r in range(CL)]
    stacked = jnp.concatenate(
        [places[m] for m in members] + [jnp.zeros((TB - 3 * CL, TB), jnp.float32)], axis=0
    )
    cols[...] = stacked.T
    live = lax.broadcasted_iota(jnp.int32, weights_ref.shape, 0) < count_ref[0, 0]
    scaled = jnp.where(live, weights_ref[...], 0.0) / point_total
    scaled = jnp.concatenate(
        [scaled, jnp.zeros((TB - batches, point_total), jnp.float32)], axis=0
    )
    wcol[...] = scaled.T

    for d in range(1, basis_size):
        f_copy(d).wait_recv()
    firsts_in = pltpu.make_async_copy(firsts, firsts_s, local_sem)
    firsts_in.start()
    for c in range(block_count):
        density_in(c).wait()
    firsts_in.wait()

    def fx_copy(k, d):
        return pltpu.make_async_remote_copy(
            src_ref=packed.at[d, k],
            dst_ref=landed[k].at[d],
            send_sem=fx_send.at[d - 1, k],
            recv_sem=fx_recv.at[d - 1, k],
            device_id=(me_grid, lax.rem(me_basis + d, basis_size)),
            device_id_type=MESH,
        )

    def fz_copy(k, j, side):
        cc, part = k // parts, k % parts
        at = (j, cc, slice(None), pl.ds(part * rows, rows))
        return pltpu.make_async_remote_copy(
            src_ref=dens.at[at],
            dst_ref=dens.at[at],
            send_sem=fz_send.at[j, k, side],
            recv_sem=fz_recv.at[j, k],
            device_id=(me_grid + 1 if side == 0 else me_grid - 1, me_basis),
            device_id_type=MESH,
        )

    def pack(k, d):
        cc, part = k // parts, k % parts
        begin = firsts_s[lax.rem(basis_size - d, basis_size), 0, 0]
        if d == 0:
            column = member(first, me_grid * per + cc)
        else:
            column = member(begin, me_grid * per + cc)
        for i in range(owned):
            block = density_v[column, i * TB + part * rows : i * TB + (part + 1) * rows, :]
            if d == 0:
                landed[k][0, i] = block
            else:
                packed[d, k, i] = block

    slots = [lax.rem(me_basis - m // owned + basis_size, basis_size) for m in members]

    def own(k):
        cc, part = k // parts, k % parts
        for d in range(1, basis_size):
            fx_copy(k, d).wait_recv()
        for r in range(CL):
            dens[me_grid, cc, r, part * rows : (part + 1) * rows, :] = landed[k][
                slots[r], r % owned
            ]

        @pl.when(me_grid < grid_size - 1)
        def _():
            fz_copy(k, me_grid, 0).start()

        @pl.when(me_grid > 0)
        def _():
            fz_copy(k, me_grid, 1).start()

    def relay(k, h):
        @pl.when(me_grid >= h)
        def _():
            fz_copy(k, me_grid - h, 0).wait_recv()

            @pl.when(me_grid < grid_size - 1)
            def _():
                fz_copy(k, me_grid - h, 0).start()

        @pl.when(me_grid + h < grid_size)
        def _():
            fz_copy(k, me_grid + h, 1).wait_recv()

            @pl.when(me_grid > 0)
            def _():
                fz_copy(k, me_grid + h, 1).start()

    sharpness = float(centers_ref.shape[1]) ** (2.0 / 3.0)

    def couple(r):
        mine = [cols[:, 3 * r + d : 3 * r + d + 1] for d in range(3)]
        for u in range(CL):
            other = places[members[u]]
            spread = [mine[d] - other[d : d + 1] for d in range(3)]
            distance = spread[0] * spread[0] + spread[1] * spread[1] + spread[2] * spread[2]
            coup[r, u] = jnp.exp(-sharpness * distance).astype(jnp.bfloat16)

    pair_shape = (lists * lists, point_total)
    t_at = lax.broadcasted_iota(jnp.int32, pair_shape, 0) // lists
    u_at = lax.broadcasted_iota(jnp.int32, pair_shape, 0) % lists

    def positions(b):
        slots_at = [lists_ref[t, b] & (CL - 1) for t in range(lists)]
        spots = []
        for r in range(CL):
            spot = jnp.int32(lists)
            for t in range(lists):
                spot = jnp.where(slots_at[t] == r, t, spot)
            spots.append(spot)
        return spots

    def weigh(b):
        spots = positions(b)
        for r in range(CL):
            wx[b * point_total : (b + 1) * point_total, r * TB : (r + 1) * TB] = (
                values_v[b, spots[r]].astype(jnp.float32) * wcol[:, b : b + 1]
            ).astype(jnp.bfloat16)
        blocks = [lists_ref[t, b] for t in range(lists)]

        def spread_out(numbers, at):
            result = jnp.full(pair_shape, numbers[0], jnp.float32)
            for t in range(1, lists):
                result = jnp.where(at == t, numbers[t], result)
            return result

        distance = None
        for d in range(3):
            numbers = [bc_ref[d, block] for block in blocks]
            middle = 0.5 * (spread_out(numbers, t_at) + spread_out(numbers, u_at))
            offset = points_ref[d, b : b + 1, :].astype(jnp.float32) - middle
            square = offset * offset
            distance = square if distance is None else distance + square
        numbers = [be_ref[block] for block in blocks]
        rate = 0.5 * (spread_out(numbers, t_at) + spread_out(numbers, u_at))
        tau = rate * distance + 0.05
        root = jnp.sqrt(tau)
        boys[b] = 0.5 * math.sqrt(math.pi) * lax.erf(root) / root

    work = [functools.partial(couple, r) for r in range(CL)]
    work += [functools.partial(weigh, b) for b in range(batches)]
    share = -(-len(work) // chunks)

    for k in range(chunks):
        for d in range(1, basis_size):
            pack(k, d)
            fx_copy(k, d).start()
    for k in range(chunks):
        pack(k, 0)
    for t in range(lists):
        values_in(t).wait()
    values_v[:, lists] = jnp.zeros((batches, point_total, TB), jnp.bfloat16)
    for k in range(chunks + grid_size):
        for piece in work[k * share : (k + 1) * share]:
            piece()
        if k < chunks:
            own(k)
        for h in range(1, grid_size):
            if 0 <= k - h < chunks:
                relay(k - h, h)

    for g in range(group):
        pots[g, lists] = jnp.zeros((TB, point_total), jnp.bfloat16)

    def potential(n, carry):
        for g in range(group):
            b = n * group + g
            at = [lists_ref[t, b] & (CL - 1) for t in range(lists)]
            tiles = jnp.concatenate(
                [
                    jnp.concatenate([dens[c // per, lax.rem(c, per), r] for c in at], axis=1)
                    for r in at
                ],
                axis=0,
            )
            listed = jnp.concatenate([values_v[b, t] for t in range(lists)], axis=1)
            mapped = lax.dot_general(
                tiles, listed, (((1,), (1,)), ((), ())), preferred_element_type=jnp.float32
            ).astype(jnp.bfloat16)
            total = None
            for u in range(lists):
                side = jnp.concatenate([coup[r, at[u]] for r in at], axis=0)
                part = jnp.dot(
                    side, mapped[u * TB : (u + 1) * TB], preferred_element_type=jnp.float32
                )
                part = jnp.concatenate(
                    [
                        part[t * TB : (t + 1) * TB] * boys[b, t * lists + u : t * lists + u + 1, :]
                        for t in range(lists)
                    ],
                    axis=0,
                )
                total = part if total is None else total + part
            total = total.astype(jnp.bfloat16)
            for t in range(lists):
                pots[g, t] = total[t * TB : (t + 1) * TB]
            spots = positions(b)
            span = pl.ds(pl.multiple_of(b * point_total, point_total), point_total)
            for c in range(CL):
                potx[c * TB : (c + 1) * TB, span] = pots[g, spots[c]]
        return carry

    lax.fori_loop(0, batches // group, potential, 0)

    def sum_up(u, j):
        side = jnp.concatenate(
            [
                wx[:, (m * owned + u) * TB : (m * owned + u + 1) * TB]
                for m in range(members_total)
            ],
            axis=1,
        )
        at = pl.ds(pl.multiple_of(j * (per * TB), per * TB), per * TB)
        total = jnp.dot(potx[at, :], side, preferred_element_type=jnp.float32)
        for i in range(per):
            for m in range(members_total):
                acc[u, j * per + i, m] = total[i * TB : (i + 1) * TB, m * TB : (m + 1) * TB]

    def pair(sources, targets, sends, recvs, device):
        return [
            pltpu.make_async_remote_copy(
                src_ref=sources[which],
                dst_ref=targets[which],
                send_sem=sends.at[which],
                recv_sem=recvs.at[which],
                device_id=device,
                device_id_type=MESH,
            )
            for which in range(2)
        ]

    def right_copy(u, j):
        return pair(
            (kq.at[j, u], ks.at[j, u]),
            (lq.at[j, u], ls.at[j, u]),
            r_send.at[j, u],
            l_recv.at[j, u],
            (lax.rem(me_grid + 1, grid_size), me_basis),
        )

    def left_copy(u, j):
        return pair(
            (kq.at[j, u], ks.at[j, u]),
            (rq.at[j, u], rs.at[j, u]),
            r_send.at[j, u],
            r_recv.at[j, u],
            (lax.rem(me_grid + grid_size - 1, grid_size), me_basis),
        )

    def x_copy(u, d):
        to = lax.rem(me_basis + d, basis_size)
        its = lax.rem(to, members_total)
        return pair(
            (sq.at[u, its], ss.at[u, its]),
            (xq.at[d - 1, u], xs.at[d - 1, u]),
            x_send.at[d - 1, u],
            x_recv.at[d - 1, u],
            (me_grid, to),
        )

    def w_place(q):
        at = CL * q + me_grid * per
        return at // per_owner, lax.rem(at, per_owner) // per

    def w_copy(u, q):
        to, slot = w_place(q)
        return pair(
            (hq.at[q, u], hs.at[q, u]),
            (wq.at[slot, u], ws.at[slot, u]),
            w_send.at[q, u],
            w_recv.at[slot, u],
            (to, me_basis),
        )

    def w_arrival(u, slot):
        return pair(
            (hq.at[slot, u], hs.at[slot, u]),
            (wq.at[slot, u], ws.at[slot, u]),
            w_send.at[slot, u],
            w_recv.at[slot, u],
            (lax.rem(me_grid + 1, grid_size), me_basis),
        )

    def w_from(slot):
        return lax.rem(me_grid * per_owner + slot * per, CL) // per

    def partial_sum(u, j, m, i):
        return acc[u, j * per + i, m]

    def pass_on(u, j, incoming):
        for m in range(members_total):
            for i in range(width):
                n = m * width + i
                total = partial_sum(u, j, m, i)
                if incoming is not None:
                    total += decode(incoming[0][j, u, n], incoming[1][j, u, pl.ds(n, 1), :])
                kq[j, u, n], ks[j, u, pl.ds(n, 1), :] = encode(total)

    def flow(u, e):
        @pl.when(me_grid + e < grid_size)
        def _():
            j = me_grid + e
            sum_up(u, j)

            @pl.when(me_grid == 0)
            def _():
                pass_on(u, j, None)

            @pl.when(me_grid > 0)
            def _():
                for copy in right_copy(u, j):
                    copy.wait_recv()
                pass_on(u, j, (lq, ls))

            for copy in right_copy(u, j):
                copy.start()

        @pl.when(me_grid - e >= 0)
        def _():
            j = me_grid - e
            sum_up(u, j)

            @pl.when(me_grid == grid_size - 1)
            def _():
                pass_on(u, j, None)

            @pl.when(me_grid < grid_size - 1)
            def _():
                for copy in left_copy(u, j):
                    copy.wait_recv()
                pass_on(u, j, (rq, rs))

            for copy in left_copy(u, j):
                copy.start()

    def settle(u):
        sum_up(u, me_grid)

        @pl.when(me_grid > 0)
        def _():
            for copy in right_copy(u, me_grid):
                copy.wait_recv()

        @pl.when(me_grid < grid_size - 1)
        def _():
            for copy in left_copy(u, me_grid):
                copy.wait_recv()

        def finish(sides):
            for m in range(members_total):
                for i in range(width):
                    n = m * width + i
                    total = partial_sum(u, me_grid, m, i)
                    for q, s in sides:
                        total += decode(q[me_grid, u, n], s[me_grid, u, pl.ds(n, 1), :])
                    sq[u, m, i], ss[u, m, pl.ds(i, 1), :] = encode(total.T)

        if grid_size == 1:
            finish([])
        else:

            @pl.when(me_grid == 0)
            def _():
                finish([(rq, rs)])

            @pl.when(me_grid == grid_size - 1)
            def _():
                finish([(lq, ls)])

            @pl.when((me_grid > 0) & (me_grid < grid_size - 1))
            def _():
                finish([(lq, ls), (rq, rs)])

        for d in range(1, basis_size):
            for copy in x_copy(u, d):
                copy.start()

    def wrap(number):
        return jnp.where(number < 0, number + block_count, number)

    def place(u):
        for d in range(1, basis_size):
            for copy in x_copy(u, d):
                copy.wait_recv()
        block = me_basis * owned + u

        def spot(i, carry):
            residue = me_grid * per + i
            totals = [None] * turns
            for d in range(basis_size):
                begin = firsts[d]
                inside = wrap(block - begin) < CL
                column = begin + ((residue - begin) & (CL - 1))
                column = jnp.where(column >= block_count, column - block_count, column)
                turn = column >> (CL.bit_length() - 1)
                if d == 0:
                    coded, scale = sq[u, mine, i], ss[u, mine, pl.ds(i, 1), :]
                else:
                    coded, scale = xq[d - 1, u, i], xs[d - 1, u, pl.ds(i, 1), :]
                number = coded.astype(jnp.int32).astype(jnp.float32)
                for q in range(turns):
                    term = number * jnp.where(inside & (turn == q), scale, 0.0)
                    totals[q] = term if totals[q] is None else totals[q] + term
            for q in range(turns):
                hq[q, u, i], hs[q, u, pl.ds(i, 1), :] = encode(totals[q])
            return carry

        lax.fori_loop(0, width, spot, 0)
        for q in range(turns):
            to, slot = w_place(q)

            @pl.when(to != me_grid)
            def _():
                for copy in w_copy(u, q):
                    copy.start()

            @pl.when(to == me_grid)
            def _():
                wq[slot, u] = hq[q, u]
                ws[slot, u] = hs[q, u]

    def out_copy(u):
        at = slice(u * TB, (u + 1) * TB)
        return pltpu.make_async_copy(out.at[at], out_hbm.at[at], out_sems.at[u])

    def deliver(u):
        for slot in range(turns):

            @pl.when(w_from(slot) != me_grid)
            def _():
                for copy in w_arrival(u, slot):
                    copy.wait_recv()

            row = u * TB
            for i in range(width):
                column = (slot * per + i) * TB
                out[row : row + TB, column : column + TB] = decode(
                    wq[slot, u, i], ws[slot, u, i : i + 1, :]
                )
        out_copy(u).start()

    hops = grid_size - 1
    for s in range(units + hops + PLACE_LAG + DELIVER_LAG):
        for e in range(hops, 0, -1):
            if 0 <= s - (hops - e) < units:
                flow(s - (hops - e), e)
        if 0 <= s - hops < units:
            settle(s - hops)
        if 0 <= s - hops - PLACE_LAG < units:
            place(s - hops - PLACE_LAG)
        if 0 <= s - hops - PLACE_LAG - DELIVER_LAG < units:
            deliver(s - hops - PLACE_LAG - DELIVER_LAG)

    for u in range(units):
        out_copy(u).wait()
        for e in range(1, grid_size):

            @pl.when(me_grid + e < grid_size)
            def _():
                for copy in right_copy(u, me_grid + e):
                    copy.wait_send()

            @pl.when(me_grid - e >= 0)
            def _():
                for copy in left_copy(u, me_grid - e):
                    copy.wait_send()

        for d in range(1, basis_size):
            for copy in x_copy(u, d):
                copy.wait_send()
        for q in range(turns):

            @pl.when(w_place(q)[0] != me_grid)
            def _():
                for copy in w_copy(u, q):
                    copy.wait_send()

    for d in range(1, basis_size):
        f_copy(d).wait_send()
    for k in range(chunks):
        for d in range(1, basis_size):
            fx_copy(k, d).wait_send()
        for h in range(grid_size):

            @pl.when((me_grid >= h) & (me_grid < grid_size - 1))
            def _():
                fz_copy(k, me_grid - h, 0).wait_send()

            @pl.when((me_grid + h < grid_size) & (me_grid > 0))
            def _():
                fz_copy(k, me_grid + h, 1).wait_send()


def exchange(
    values, weights, points, block_lists, counts, density, centers, block_centers, block_exponents,
    grid_size, basis_size,
):
    per = CL // grid_size
    parts = 8 // per
    chunks = per * parts
    batches, point_total, listed = values.shape
    lists = block_lists.shape[1]
    block_count = block_exponents.shape[0]
    owned = block_count // basis_size
    turns = block_count // CL
    members = CL // owned
    group = math.gcd(batches, 8)
    f32, bf16, i32 = jnp.float32, jnp.bfloat16, jnp.int32
    hbm = pl.BlockSpec(memory_space=pltpu.HBM)
    dma = pltpu.SemaphoreType.DMA

    def both(*lead):
        return [pltpu.VMEM(lead + (TB, TB), jnp.int16), pltpu.VMEM(lead + (TB,), f32)]

    scratch = [
        pltpu.VMEM((owned * TB, turns * per * TB), f32),
        dma((owned,)),
        pltpu.VMEM((batches, lists + 1, point_total, TB), bf16),
        pltpu.VMEM((block_count, density.shape[0], TB), bf16),
        pltpu.VMEM((basis_size, chunks, owned, TB // parts, TB), bf16),
        pltpu.VMEM((grid_size, per, CL, TB, TB), bf16),
        pltpu.VMEM((CL, CL, TB, TB), bf16),
        pltpu.VMEM((batches, lists * lists, point_total), f32),
        pltpu.VMEM((batches * point_total, CL * TB), bf16),
        pltpu.VMEM((group, lists + 1, TB, point_total), bf16),
        pltpu.VMEM((CL * TB, batches * point_total), bf16),
        pltpu.VMEM((owned, CL, members, TB, TB), f32),
        pltpu.VMEM((basis_size, 1, TB), i32),
        pltpu.VMEM((1, TB), i32),
        pltpu.SMEM((basis_size, 1, TB), i32),
        pltpu.VMEM((point_total, TB), f32),
        pltpu.VMEM((TB, TB), f32),
        pltpu.VMEM((block_count, 3, TB), f32),
        pltpu.SMEM((lists, batches), i32),
        pltpu.SMEM((1, 1), i32),
        pltpu.SMEM(block_centers.shape, f32),
        pltpu.SMEM(block_exponents.shape, f32),
        pltpu.VMEM(weights.shape, f32),
        pltpu.VMEM((3, batches, point_total), bf16),
        pltpu.VMEM(centers.shape, f32),
    ]
    scratch += both(grid_size, owned, members * per) * 3
    scratch += both(owned, members, per) + both(basis_size - 1, owned, per)
    scratch += both(turns, owned, per) * 2
    scratch += [dma((7,)), dma(()), dma((block_count,)), dma((lists,))]
    scratch += [dma((basis_size - 1,))] * 2 + [dma((basis_size - 1, chunks))] * 2
    scratch += [dma((grid_size, chunks, 2)), dma((grid_size, chunks))]
    scratch += [dma((grid_size, owned, 2))] * 3 + [dma((basis_size - 1, owned, 2))] * 2
    scratch += [dma((turns, owned, 2))] * 2
    scratch += [pltpu.VMEM((basis_size, owned, TB // parts, TB), bf16) for k in range(chunks)]
    return pl.pallas_call(
        functools.partial(
            exchange_kernel, grid_size, basis_size, owned, turns, parts, group
        ),
        out_shape=jax.ShapeDtypeStruct((owned * TB, turns * per * TB), f32),
        in_specs=[hbm] * 9,
        out_specs=hbm,
        scratch_shapes=scratch,
        compiler_params=pltpu.CompilerParams(
            collective_id=0, has_side_effects=True, vmem_limit_bytes=58 * 1024 * 1024
        ),
        name="exchange",
    )(
        block_lists.T, counts, block_centers, block_exponents, weights,
        points.transpose(1, 0, 2), centers, values, density,
    )


def body(*arrays):
    return exchange(*arrays, lax.axis_size("grid"), lax.axis_size("basis"))


def solution(mesh):
    placed = (
        P(("grid", "basis"), None, None),
        P(("grid", "basis"), None),
        P(("grid", "basis"), None, None),
        P(("grid", "basis"), None),
        P("basis", "grid"),
        P("basis", None),
        P(),
        P(),
        P(),
    )
    return jax.shard_map(
        body, mesh=mesh, in_specs=placed, out_specs=P("basis", "grid"), check_vma=False
    )
```
